512 devices in a mesh: lon: 32 (over x, z_lo), lat: 16 (over y, z_hi, core).
Axes of the slice: x: 4, y: 4, z: 16 (z_hi: 2, z_lo: 8; z = z_hi * 8 + z_lo), core: 2. Of those that a mesh axis runs over, the one named last changes fastest.
Arguments:
- increment: bfloat16 [2, 127, 128, 4096], P(None, None, 'lat', 'lon'), may hold values from -6 to 6
- std_dev: bfloat16 [2, 127, 128, 4096], P(None, None, 'lat', 'lon'), may hold values from 0.5 to 4
- level_group: int32 [127], replicated, may hold values from 0 to 3, never falling along the last dimension, each value on 1 to 40 neighbouring positions
- lon_reach: float32 [2, 4, 4], replicated, may hold values from 8 to 16384
- lon_weight: float32 [2, 4, 4], replicated, may hold values from 0.2 to 1
- lat_reach: float32 [2, 4, 4], replicated, may hold values from 2 to 512
- lat_weight: float32 [2, 4, 4], replicated, may hold values from 0.2 to 1
- vertical: float32 [2, 127, 127], replicated, may hold values from -0.5 to 0.5
Outputs:
- covaried: bfloat16 [2, 127, 128, 4096], P(None, None, 'lat', 'lon')
The draws below stay inside these ranges and needn't reach their ends.
Inputs may be any that keep to these rules, and one draw needn't show every extreme that they name: level_group never falls along the levels; each of the 4 groups holds 1 to 40 consecutive levels and one holds exactly 40.
All inputs are finite; a program needn't handle non-finite values.
Results may differ from the reference program's by a relative error of at most 0.003.
Values sent between devices are 32-bit elements; how exact they have to be, the bound alone decides.
A program may use at most 64 MiB of HBM per device.

```python
import math
import jax
import jax.numpy as jnp
import numpy as np
from jax import lax

V = 2
K = 127
NB = 4
MOST = 40
NLAT = 128
NLON = 4096


def block_levels(rng, dims, cuts, least, top_value):
    def one(position, shards_of):
        steps = jax.random.uniform(jax.random.fold_in(jax.random.fold_in(rng, 6), position), (shards_of,), jnp.float32, least / len(cuts), top_value / len(cuts))
        return jnp.repeat(jnp.exp(steps), dims[position] // shards_of).reshape((-1,) + (1,) * (len(dims) - position - 1))

    gain = one(*cuts[0])
    for cut in cuts[1:]:
        gain = gain * one(*cut)
    return gain


def profile(amount, total, bound, slope):
    loads = [(1 << 20) // math.isqrt(rank ** slope) + 1 for rank in range(2, amount + 1)]
    rest, holding = total - bound - (amount - 1), [1] * (amount - 1)
    while rest > 0:
        candidates = [i for i in range(amount - 1) if holding[i] < bound]
        pool, left = sum([loads[i] for i in candidates]), rest
        for i in candidates:
            more = min(bound - holding[i], max(1, left * loads[i] // pool), rest)
            holding[i] = holding[i] + more
            rest = rest - more
    return np.array([bound] + holding)


def uneven_parts(stream_key, number_of, total, reach, skew):
    if number_of == 2:
        one = jax.random.randint(stream_key, (), max(1, total - reach), min(reach, total - 1) + 1)
        return jnp.stack([one, total - one])
    sizes = jnp.asarray(profile(number_of, total, reach, skew), jnp.int32)
    twos = (number_of - 1) // 2
    source_of, taker = sizes[1:1 + 2 * twos:2], sizes[2:2 + 2 * twos:2]
    room = jnp.minimum(source_of - 1, reach - taker)
    shifted = jax.random.randint(jax.random.fold_in(stream_key, 1), (twos,), 0, 1 << 20) % (room + 1)
    sizes = sizes.at[1:1 + 2 * twos:2].set(source_of - shifted).at[2:2 + 2 * twos:2].set(taker + shifted)
    return sizes[jax.random.permutation(jax.random.fold_in(stream_key, 2), number_of)]


def bell_draw(own_key, shape, scale, most, pieces=(), dtype=jnp.bfloat16):
    values = jax.random.normal(own_key, shape, jnp.float32) * scale
    if len(pieces) > 0:
        values = block_levels(own_key, shape, pieces, -0.22, 0.18) * values
    return jnp.clip(values, min=-most, max=most).astype(dtype)


def setup_inputs(seed: int = 0) -> dict:
    keys = jax.random.split(jax.random.key(seed), 9)
    return {
        "increment": bell_draw(keys[0], (V, K, NLAT, NLON), 1.0, 6.0, ((2, 16), (3, 32))),
        "std_dev": jnp.clip(jnp.exp(math.log(4.0) - 2.0794415 * jax.random.uniform(keys[1], (V, K, NLAT, NLON), jnp.float32) ** block_levels(keys[1], (V, K, NLAT, NLON), ((2, 16), (3, 32)), -0.2, 0.2)), 0.5, 4.0).astype(jnp.bfloat16),
        "level_group": jnp.searchsorted(jnp.cumsum(uneven_parts(keys[2], NB, K, MOST, 0)), jnp.arange(K), side="right").astype(jnp.int32),
        "lon_reach": jnp.clip(jnp.exp(jax.random.uniform(keys[3], (V, NB, 4), jnp.float32, math.log(8.0), math.log(16384.0))), 8.0, 16384.0),
        "lon_weight": jnp.clip(jax.random.uniform(keys[4], (V, NB, 4), jnp.float32, 0.2, 1.0), 0.2, 1.0),
        "lat_reach": jnp.clip(jnp.exp(jax.random.uniform(keys[5], (V, NB, 4), jnp.float32, math.log(2.0), math.log(512.0))), 2.0, 512.0),
        "lat_weight": jnp.clip(jax.random.uniform(keys[6], (V, NB, 4), jnp.float32, 0.2, 1.0), 0.2, 1.0),
        "vertical": bell_draw(keys[7], (V, K, K), K ** -0.5, 0.5, (), jnp.float32),
    }


def recurse(inputs, rates, weights):
    def advance(memory, current_row):
        memory = current_row[None, :] + rates[:, None] * memory
        return memory, jnp.sum(weights[:, None] * memory, axis=0)

    start_state = jnp.zeros((rates.shape[0], inputs.shape[1]), jnp.float32)
    _, outputs = lax.scan(advance, start_state, inputs)
    return outputs


def periodic(inputs, inverse, weights):
    rates = jnp.exp(-inverse)
    length = inputs.shape[0]

    def advance(memory, current_row):
        memory = current_row[None, :] + rates[:, None] * memory
        return memory, memory

    start_state = jnp.zeros((rates.shape[0], inputs.shape[1]), jnp.float32)
    _, states = lax.scan(advance, start_state, inputs)
    closure = -jnp.expm1(-(length * 1.0) * inverse)
    closing = states[-1] / closure[:, None]
    steps = (jnp.arange(length) + 1).astype(jnp.float32)
    tail = jnp.exp(-steps[:, None] * inverse[None, :])
    whole = states + tail[:, :, None] * closing[None, :, :]
    return jnp.sum(weights[None, :, None] * whole, axis=1)


def filter_level(bundle):
    slab, inverse_lon, weights_lon, inverse_lat, weights_lat = bundle
    columns = jnp.transpose(slab)
    eastward = periodic(columns, inverse_lon, weights_lon)
    westward = periodic(eastward[::-1], inverse_lon, weights_lon)[::-1]
    eastwest = jnp.transpose(westward)
    rates_lat = jnp.exp(-inverse_lat)
    northward = recurse(eastwest, rates_lat, weights_lat)
    southward = recurse(northward[::-1], rates_lat, weights_lat)[::-1]
    return southward


def reference(increment, std_dev, level_group, lon_reach, lon_weight, lat_reach, lat_weight, vertical):
    spread_dev = std_dev.astype(jnp.float32)
    scaled = spread_dev * increment.astype(jnp.float32)
    inverse_lon = 1.0 / lon_reach[:, level_group, :]
    weights_lon = lon_weight[:, level_group, :] * (1.0 - jnp.exp(-inverse_lon))
    inverse_lat = 1.0 / lat_reach[:, level_group, :]
    weights_lat = lat_weight[:, level_group, :] * (1.0 - jnp.exp(-inverse_lat))
    variables, levels, height, cells = scaled.shape
    slabs = scaled.reshape(variables * levels, height, cells)
    filtered = lax.map(filter_level, (slabs, inverse_lon.reshape(-1, 4), weights_lon.reshape(-1, 4),
                                      inverse_lat.reshape(-1, 4), weights_lat.reshape(-1, 4)))
    filtered = filtered.reshape(variables, levels, height, cells)
    mixed = jnp.einsum('vkj,vjal->vkal', vertical, filtered, precision=lax.Precision.HIGHEST)
    return (spread_dev * mixed).astype(jnp.bfloat16)
```

```python
import functools

import jax
import jax.numpy as jnp
from jax import lax
from jax.experimental import pallas as pl
from jax.experimental.pallas import tpu as pltpu
from jax.sharding import PartitionSpec as P

MOST = 40
KP = 128
MESH = pl.DeviceIdType.MESH
HI = lax.Precision.HIGHEST
AHEAD = 3


def place():
    lon = lax.axis_index("lon")
    lat = lax.axis_index("lat")
    return lon // 8, lon % 8, lat // 4, (lat // 2) % 2, lat % 2


def target(x, z_lo, y, z_hi, core):
    return {"lon": x * 8 + z_lo, "lat": y * 4 + z_hi * 2 + core}


def tables(level_group, lon_reach, lon_weight, lat_reach, lat_weight, rows, cells, nlat, nlon):
    band = lax.axis_index("lat")
    groups = lon_reach.shape[1]
    pick = level_group[None, :] == jnp.arange(groups, dtype=jnp.int32)[:, None]

    def by_level(grouped):
        parts = [jnp.where(pick[g], grouped[:, g][..., None], 0.0) for g in range(groups)]
        return functools.reduce(jnp.add, parts)

    inv_lat = 1.0 / lat_reach
    coef_lat = lat_weight * (1.0 - jnp.exp(-inv_lat))
    row = jnp.arange(rows, dtype=jnp.float32)
    left = (nlat - band * rows).astype(jnp.float32) - row
    both = inv_lat[..., :, None] + inv_lat[..., None, :]
    ratio = jnp.expm1(-both[..., None] * left) / jnp.expm1(-both)[..., None]
    gain = coef_lat[..., None] * jnp.sum(coef_lat[:, :, None, :, None] * ratio, axis=3)
    inv = inv_lat[..., None]
    take_f = jnp.exp(-(rows - 1.0 - row) * inv)
    take_b = jnp.exp(-row * inv) * gain
    take = jnp.stack([take_f, take_b], axis=2)
    give_f = jnp.swapaxes(gain * jnp.exp(-(row + 1.0) * inv), 2, 3)
    give_b = jnp.swapaxes(jnp.exp(-(rows - row) * inv), 2, 3)
    gap = jnp.abs(row[:, None] - row[None, :])
    later = jnp.maximum(row[:, None], row[None, :]).astype(jnp.int32)
    local = jnp.sum(jnp.exp(-gap * inv[..., None]) * gain[..., later], axis=2)

    lanes_j = KP // rows
    take_pat = jnp.tile(jnp.concatenate([take, take], axis=3), (1, 1, 1, 1, lanes_j))
    local_pat = jnp.tile(local, (1, 1, 1, lanes_j))
    give_pat = jnp.concatenate([jnp.tile(give_f, (1, 1, 1, lanes_j)), jnp.tile(give_b, (1, 1, 1, lanes_j))], axis=3)
    apply_pat = jnp.concatenate([local_pat, give_pat], axis=3)
    step_lat = jnp.exp(-rows * inv_lat)
    step_pat = jnp.broadcast_to(jnp.concatenate([step_lat, step_lat], axis=2)[..., None], step_lat.shape[:2] + (8, KP))

    inv_lon = 1.0 / lon_reach
    coef_lon = lon_weight * (1.0 - jnp.exp(-inv_lon))
    pair = inv_lon[..., :, None] + inv_lon[..., None, :]
    amp = coef_lon * jnp.sum(coef_lon[:, :, None, :] / -jnp.expm1(-pair), axis=3)
    cell = jnp.arange(cells, dtype=jnp.float32)
    inv = inv_lon[..., None]
    edge = jnp.concatenate([jnp.exp(-(cells - 1.0 - cell) * inv), jnp.exp(-cell * inv)], axis=2)
    decay = jnp.concatenate([amp[..., None] * jnp.exp(-(cell + 1.0) * inv), amp[..., None] * jnp.exp(-(cells - cell) * inv)], axis=2)
    span = jnp.abs(cell[:, None] - cell[None, :])
    inside = jnp.sum(amp[..., None, None] * jnp.exp(-span * inv[..., None]), axis=2)
    vs = edge.shape[0]
    edge = edge.reshape(vs, groups * 8, cells)
    decay = decay.reshape(vs, groups * 8, cells)

    inv8 = by_level(jnp.concatenate([inv_lon, inv_lon], axis=2))
    closing = 1.0 / -jnp.expm1(-nlon * inv8)
    step_lane = jnp.broadcast_to(by_level(step_lat)[:, :, None, :], (vs, 4, 8, KP))
    take_lane = by_level(take.reshape(vs, groups, 8, rows))
    local_lane = by_level(local)
    give_lane = by_level(jnp.concatenate([give_f, give_b], axis=3))
    return dict(take_pat=take_pat, apply_pat=apply_pat, step_pat=step_pat, edge=edge, decay=decay, inside=inside,
                inv8=inv8, closing=closing, step_lane=step_lane, take_lane=take_lane, local_lane=local_lane, give_lane=give_lane)


def moments_kernel(group_ref, inc_ref, std_ref, row_ref, take_ref, step_ref, edge_ref, m_ref, me_ref, r8_ref, x_ref, bd_ref):
    vs, levels = inc_ref.shape[0], inc_ref.shape[1]
    lane = lax.broadcasted_iota(jnp.int32, (8, KP), 1) // 8
    low = lax.broadcasted_iota(jnp.int32, (8, KP), 0) < 4
    for v in range(vs):
        product = inc_ref[v].astype(jnp.float32) * std_ref[v].astype(jnp.float32)
        x_ref[v, pl.ds(0, levels * 8)] = product.reshape(levels * 8, KP)
        x_ref[v, pl.ds(levels * 8, 8 * (KP - levels))] = jnp.zeros((8 * (KP - levels), KP), jnp.float32)

    def build(t, carry):
        g0, g1 = group_ref[2 * t], group_ref[2 * t + 1]
        block, sub = t // 8, t % 8
        own = jnp.where(low, 2 * sub, 2 * sub + 1) == lane
        for v in range(vs):
            r8_ref[v, block, sub] = jnp.where(low, step_ref[v, g0], step_ref[v, g1])
            for part in range(2):
                tile = jnp.where(own, jnp.where(low, take_ref[v, g0, part], take_ref[v, g1, part]), 0.0)
                bd_ref[v, block, pl.ds(pl.multiple_of(part * 64 + sub * 8, 8), 8)] = tile
        return carry

    lax.fori_loop(0, KP // 2, build, 0)
    for v in range(vs):
        for block in range(8):
            out = jnp.dot(bd_ref[v, block], x_ref[v, pl.ds(block * 128, 128)], precision=HI, preferred_element_type=jnp.float32)
            m_ref[block // 4, v * 4 + block % 4] = out.reshape(2, 8, 8, KP)
        for i in range(8):
            rows = x_ref[v, pl.ds(i, KP, stride=8)]
            sums = lax.dot_general(edge_ref[v], rows, (((1,), (1,)), ((), ())), precision=HI, preferred_element_type=jnp.float32)
            me_ref[v, i] = functools.reduce(jnp.add, [jnp.where(row_ref[...] == g, sums[8 * g:8 * g + 8], 0.0) for g in range(4)])


def exchange_kernel(m_ref, me_ref, r8_ref, step_ref, take_ref, inv_ref, closing_ref,
                    w_ref, wu_ref, u_ref,
                    d1_ref, pm_ref, zr_ref, q_ref, yr_ref, ws_ref,
                    ud1_ref, um_ref, upm_ref, uzr_ref, uq_ref, uyr_ref, uws_ref,
                    ts_ref, tr_ref, xr_ref,
                    d1s, d1r, zss, zrs, yss, yrs, d2s, d2r, ls, lr, xs, xrs):
    x, z_lo, y, z_hi, core = place()
    chunks = m_ref.shape[1]
    mate = target(x, z_lo, y, z_hi, 1 - core)
    across = target(x, z_lo, y, 1 - z_hi, core)
    ys = [target(x, z_lo, (y + d) % 4, z_hi, core) for d in (1, 2, 3)]
    xs_to = [target((x + d) % 4, z_lo, y, z_hi, core) for d in (1, 2, 3)]
    cubes = []
    for m in (1, 2, 4):
        bit = (z_lo // m) % 2
        cubes.append((m, bit, target(x, z_lo + m - 2 * m * bit, y, z_hi, core)))
    partners = [mate, across] + ys + xs_to + [c[2] for c in cubes]
    barrier = pltpu.get_barrier_semaphore()
    for p in partners:
        pl.semaphore_signal(barrier, inc=1, device_id=p, device_id_type=MESH)
    pl.semaphore_wait(barrier, len(partners))

    def remote(src, dst, s, r, to):
        return pltpu.make_async_remote_copy(src_ref=src, dst_ref=dst, send_sem=s, recv_sem=r, device_id=to, device_id_type=MESH)

    def d1(c):
        return remote(m_ref.at[1 - core, c], d1_ref.at[c], d1s.at[c], d1r.at[c], mate)

    def zc(c):
        return remote(pm_ref.at[c], zr_ref.at[c], zss.at[c], zrs.at[c], across)

    def yc(c, d):
        part = (y + d) // 4
        return remote(q_ref.at[c, part], yr_ref.at[c, d - 1], yss.at[c, d - 1], yrs.at[c, d - 1], ys[d - 1])

    def d2(c):
        return remote(ws_ref.at[c], w_ref.at[core, c], d2s.at[c], d2r.at[c], mate)

    last = chunks
    ud1 = remote(um_ref.at[1 - core], ud1_ref, d1s.at[last], d1r.at[last], mate)
    uz = remote(upm_ref, uzr_ref, zss.at[last], zrs.at[last], across)
    uy = [remote(uq_ref.at[(y + d) // 4], uyr_ref.at[d - 1], yss.at[last, d - 1], yrs.at[last, d - 1], ys[d - 1]) for d in (1, 2, 3)]
    ud2 = remote(uws_ref, wu_ref.at[core], d2s.at[last], d2r.at[last], mate)

    def weigh(first, r, own, other):
        a = jnp.where(first, r, 1.0)
        b = jnp.where(first, 1.0, r)
        return a * own[0] + b * other[0], b * own[1] + a * other[1]

    def finish(r8, own, part, zr, slots):
        r16 = r8 * r8
        r32 = r16 * r16
        powers = [jnp.ones_like(r32), r32, r32 * r32]
        wf = jnp.zeros_like(r8)
        wb = jnp.zeros_like(r8)
        for d in (1, 2, 3):
            before = y >= d
            wf = wf + jnp.where(before, powers[d - 1] * slots[d - 1], 0.0)
            wb = wb + jnp.where(before, 0.0, powers[3 - d] * slots[d - 1])
        lower = z_hi == 0
        wf, wb = jnp.where(lower, wf, r16 * wf + zr[0]), jnp.where(lower, r16 * wb + zr[1], wb)
        first = core == 0
        far_f, far_b = r8 * wf, r8 * wb
        mine = jnp.where(first, wf, far_f + part[0]), jnp.where(first, far_b + part[1], wb)
        theirs = jnp.where(first, far_f + own[0], wf), jnp.where(first, wb, far_b + own[1])
        return mine, theirs

    def rate(c):
        return r8_ref[c // 4, core * 4 + c % 4]

    def stage_z(c):
        d1(c).wait_recv()
        f, b = weigh(core == 0, rate(c), (m_ref[core, c, 0], m_ref[core, c, 1]), (d1_ref[c, 0], d1_ref[c, 1]))
        pm_ref[c, 0] = f
        pm_ref[c, 1] = b
        zc(c).start()

    def stage_y(c):
        zc(c).wait_recv()
        r8 = rate(c)
        f, b = weigh(z_hi == 0, r8 * r8, (pm_ref[c, 0], pm_ref[c, 1]), (zr_ref[c, 0], zr_ref[c, 1]))
        q_ref[c, 0] = f
        q_ref[c, 1] = b
        for d in (1, 2, 3):
            yc(c, d).start()

    def stage_w(c):
        for d in (1, 2, 3):
            yc(c, d).wait_recv()
        mine, theirs = finish(rate(c), (m_ref[core, c, 0], m_ref[core, c, 1]), (d1_ref[c, 0], d1_ref[c, 1]),
                              (zr_ref[c, 0], zr_ref[c, 1]), [yr_ref[c, d] for d in range(3)])
        w_ref[core, c, 0] = mine[0]
        w_ref[core, c, 1] = mine[1]
        ws_ref[c, 0] = theirs[0]
        ws_ref[c, 1] = theirs[1]
        d2(c).start()

    def loop(start, stop, body):
        def step(c, carry):
            body(c)
            return carry
        lax.fori_loop(start, stop, step, 0)

    def lon_send(k, to):
        return remote(ts_ref.at[k], tr_ref.at[k], ls.at[k], lr.at[k], to)

    lon0 = remote(me_ref, tr_ref.at[0], ls.at[0], lr.at[0], cubes[0][2])
    lon0.start()
    loop(0, chunks, lambda c: d1(c).start())
    loop(0, AHEAD, stage_z)

    is_f = lax.broadcasted_iota(jnp.int32, (1, 1, 8, KP), 2) < 4
    inv = inv_ref[...][:, None]
    total = me_ref[...]
    prefix = jnp.zeros_like(total)
    copies = [lon0, lon_send(1, cubes[1][2]), lon_send(2, cubes[2][2])]
    for k, (m, bit, to) in enumerate(cubes):
        copies[k].wait_recv()
        other = tr_ref[k]
        upper = bit == 1
        offset = z_lo % m
        gate = jnp.where(is_f == upper, 1.0, 0.0)
        reach = jnp.where(is_f, offset, m - 1 - offset).astype(jnp.float32)
        prefix = prefix + gate * jnp.exp(-128.0 * reach * inv) * other
        whole = jnp.exp(-128.0 * m * inv)
        total = jnp.where(is_f == upper, 1.0, whole) * total + jnp.where(is_f == upper, whole, 1.0) * other
        ts_ref[k + 1] = total
        if k < 2:
            copies[k + 1].start()
        else:
            xcopies = [remote(ts_ref.at[3], xr_ref.at[d], xs.at[d], xrs.at[d], xs_to[d]) for d in range(3)]
            for cp in xcopies:
                cp.start()
        stage_y(k)
        stage_z(k + AHEAD)
    for cp in xcopies:
        cp.wait_recv()
    r1 = jnp.exp(-1024.0 * inv)
    powers = [jnp.ones_like(r1), r1, r1 * r1]
    circle = powers[2] * r1 * total
    for d in range(3):
        circle = circle + jnp.where(is_f, powers[d], powers[2 - d]) * xr_ref[d]
    reach = jnp.where(is_f, z_lo, 7 - z_lo).astype(jnp.float32)
    u_ref[...] = prefix + jnp.exp(-128.0 * reach * inv) * closing_ref[...][:, None] * circle
    for v in range(2):
        for m in range(8):
            acc = take_ref[v, m, 0:1] * u_ref[v, 0]
            for j in range(1, 8):
                acc = acc + take_ref[v, m, j:j + 1] * u_ref[v, j]
            um_ref[v, m // 4, m % 4] = acc
    ud1.start()
    stage_y(3)
    stage_z(6)
    stage_z(7)
    ud1.wait_recv()
    r8u = step_ref[core]
    own_u = (um_ref[core, 0], um_ref[core, 1])
    part_u = (ud1_ref[0], ud1_ref[1])
    f, b = weigh(core == 0, r8u, own_u, part_u)
    upm_ref[0] = f
    upm_ref[1] = b
    uz.start()
    loop(0, 3, stage_w)

    def tail(c, carry):
        stage_y(c)
        stage_w(c - 1)
        return carry

    lax.fori_loop(4, chunks, tail, 0)
    uz.wait_recv()
    zu = (uzr_ref[0], uzr_ref[1])
    f, b = weigh(z_hi == 0, r8u * r8u, (upm_ref[0], upm_ref[1]), zu)
    uq_ref[0] = f
    uq_ref[1] = b
    for cp in uy:
        cp.start()
    stage_w(chunks - 1)
    for cp in uy:
        cp.wait_recv()
    mine, theirs = finish(r8u, own_u, part_u, zu, [uyr_ref[d] for d in range(3)])
    wu_ref[core, 0] = mine[0]
    wu_ref[core, 1] = mine[1]
    uws_ref[0] = theirs[0]
    uws_ref[1] = theirs[1]
    ud2.start()

    def drain(c, carry):
        d1(c).wait_send()
        zc(c).wait_send()
        for d in (1, 2, 3):
            yc(c, d).wait_send()
        d2(c).wait()
        return carry

    lax.fori_loop(0, chunks, drain, 0)
    for cp in copies + xcopies + [ud1, uz] + uy:
        cp.wait_send()
    ud2.wait()


def apply_kernel(group_ref, start_ref, inc_ref, std_ref, row_ref, w_ref, wu_ref, u_ref, inside_ref, decay_ref, apply_ref,
                 local_ref, give_ref, vertical_ref, out_ref, x_ref, bd_ref, z_ref, y_ref, uz_ref):
    vs, levels = inc_ref.shape[0], inc_ref.shape[1]
    lane = lax.broadcasted_iota(jnp.int32, (8, 256), 1)
    lane = jnp.where(lane < 128, lane // 8, (lane % 64) // 4)
    for v in range(vs):
        product = inc_ref[v].astype(jnp.float32) * std_ref[v].astype(jnp.float32)
        x_ref[v, pl.ds(0, levels * 8)] = product.reshape(levels * 8, KP)
        x_ref[v, pl.ds(levels * 8, 8 * (KP - levels))] = jnp.zeros((8 * (KP - levels), KP), jnp.float32)

    def build(k, carry):
        g = group_ref[k]
        own = lane == k % 16
        for v in range(vs):
            bd_ref[v, pl.ds(pl.multiple_of(k * 8, 8), 8)] = jnp.where(own, apply_ref[v, g], 0.0)
        return carry

    lax.fori_loop(0, KP, build, 0)
    for v in range(vs):
        for block in range(8):
            states = w_ref[block // 4, v * 4 + block % 4].reshape(128, KP)
            source = jnp.concatenate([x_ref[v, pl.ds(block * 128, 128)], states], axis=0)
            z_ref[v, pl.ds(block * 128, 128)] = jnp.dot(bd_ref[v, pl.ds(block * 128, 128)], source, precision=HI, preferred_element_type=jnp.float32)
        z_ref[v, pl.ds(8 * KP, 8 * MOST)] = jnp.zeros((8 * MOST, KP), jnp.float32)
        y_ref[v, pl.ds(8 * levels, 8 * (KP - levels))] = jnp.zeros((8 * (KP - levels), KP), jnp.float32)
        for g in range(4):
            window = pl.ds(pl.multiple_of(start_ref[g] * 8, 8), 8 * MOST)
            y_ref[v, window] = jnp.dot(z_ref[v, window], inside_ref[v, g], precision=HI, preferred_element_type=jnp.float32)
        for i in range(8):
            acc = local_ref[v, i, 0:1] * u_ref[v, 0]
            for j in range(1, 8):
                acc = acc + local_ref[v, i, j:j + 1] * u_ref[v, j]
            for m in range(8):
                acc = acc + give_ref[v, i, m:m + 1] * wu_ref[v, m // 4, m % 4]
            for g in range(4):
                uz_ref[pl.ds(8 * g, 8)] = jnp.where(row_ref[...] == g, acc, 0.0)
            carried = lax.dot_general(uz_ref[...], decay_ref[v], (((0,), (0,)), ((), ())), precision=HI, preferred_element_type=jnp.float32)
            filtered = y_ref[v, pl.ds(i, KP, stride=8)] + carried
            x_ref[v, pl.ds(i, KP, stride=8)] = jnp.dot(vertical_ref[v], filtered, precision=HI, preferred_element_type=jnp.float32)
        mixed = x_ref[v, pl.ds(0, levels * 8)].reshape(levels, 8, KP)
        out_ref[v] = (std_ref[v].astype(jnp.float32) * mixed).astype(jnp.bfloat16)


def per_device(nlat, nlon, increment, std_dev, level_group, lon_reach, lon_weight, lat_reach, lat_weight, vertical):
    vs, levels, rows, cells = increment.shape
    f32 = jnp.float32
    groups = jnp.pad(level_group, (0, KP - levels), mode="edge")
    t = tables(groups, lon_reach, lon_weight, lat_reach, lat_weight, rows, cells, nlat, nlon)
    group_row = groups[None, :]
    starts = jnp.sum((level_group[None, :] < jnp.arange(4, dtype=jnp.int32)[:, None]).astype(jnp.int32), axis=1)
    square = jnp.pad(vertical, ((0, 0), (0, KP - levels), (0, KP - levels)))
    vmem = pl.BlockSpec(memory_space=pltpu.VMEM)
    smem = pl.BlockSpec(memory_space=pltpu.SMEM)
    limit = 48 << 20

    m, me, r8 = pl.pallas_call(
        moments_kernel,
        out_shape=(jax.ShapeDtypeStruct((2, 8, 2, 8, 8, KP), f32), jax.ShapeDtypeStruct((vs, 8, 8, KP), f32),
                   jax.ShapeDtypeStruct((vs, 8, 8, 8, KP), f32)),
        in_specs=[smem] + [vmem] * 6,
        out_specs=(vmem,) * 3,
        scratch_shapes=[pltpu.VMEM((vs, 8 * KP, KP), f32), pltpu.VMEM((vs, 8, 128, KP), f32)],
        compiler_params=pltpu.CompilerParams(vmem_limit_bytes=limit),
        name="moments",
    )(groups, increment, std_dev, group_row, t["take_pat"], t["step_pat"], t["edge"])

    dma = pltpu.SemaphoreType.DMA
    chunk = (2, 8, 8, KP)
    small = (2, 4, 8, KP)
    w, wu, u = pl.pallas_call(
        exchange_kernel,
        out_shape=(jax.ShapeDtypeStruct((2, 8) + chunk, f32), jax.ShapeDtypeStruct((vs,) + small, f32),
                   jax.ShapeDtypeStruct((vs, 8, 8, KP), f32)),
        in_specs=[vmem] * 7,
        out_specs=(vmem,) * 3,
        scratch_shapes=[
            pltpu.VMEM((8,) + chunk, f32), pltpu.VMEM((8,) + chunk, f32), pltpu.VMEM((8,) + chunk, f32),
            pltpu.VMEM((8,) + chunk, f32), pltpu.VMEM((8, 3) + chunk[1:], f32), pltpu.VMEM((8,) + chunk, f32),
            pltpu.VMEM(small, f32), pltpu.VMEM((vs,) + small, f32), pltpu.VMEM(small, f32), pltpu.VMEM(small, f32),
            pltpu.VMEM(small, f32), pltpu.VMEM((3,) + small[1:], f32), pltpu.VMEM(small, f32),
            pltpu.VMEM((4, vs, 8, 8, KP), f32), pltpu.VMEM((3, vs, 8, 8, KP), f32), pltpu.VMEM((3, vs, 8, 8, KP), f32),
            dma((9,)), dma((9,)), dma((9,)), dma((9,)), dma((9, 3)), dma((9, 3)), dma((9,)), dma((9,)),
            dma((3,)), dma((3,)), dma((3,)), dma((3,)),
        ],
        compiler_params=pltpu.CompilerParams(collective_id=0, has_side_effects=True, vmem_limit_bytes=limit),
        name="exchange",
    )(m, me, r8, t["step_lane"], t["take_lane"], t["inv8"], t["closing"])

    return pl.pallas_call(
        apply_kernel,
        out_shape=jax.ShapeDtypeStruct(increment.shape, jnp.bfloat16),
        in_specs=[smem, smem] + [vmem] * 12,
        out_specs=vmem,
        scratch_shapes=[pltpu.VMEM((vs, 8 * KP, KP), f32), pltpu.VMEM((vs, 8 * KP, 256), f32), pltpu.VMEM((vs, 8 * (KP + MOST), KP), f32),
                        pltpu.VMEM((vs, 8 * (KP + MOST), KP), f32), pltpu.VMEM((32, KP), f32)],
        compiler_params=pltpu.CompilerParams(vmem_limit_bytes=limit),
        name="apply",
    )(groups, starts, increment, std_dev, group_row, w, wu, u, t["inside"], t["decay"], t["apply_pat"],
      t["local_lane"], t["give_lane"], square)


def solution(mesh):
    placed = (P(None, None, "lat", "lon"),) * 2 + (P(),) * 6

    def whole(increment, *rest):
        nlat, nlon = increment.shape[2:]
        body = functools.partial(per_device, nlat, nlon)
        return jax.shard_map(body, mesh=mesh, in_specs=placed, out_specs=P(None, None, "lat", "lon"), check_vma=False)(increment, *rest)

    return whole
```

```python
import functools

import jax
import jax.numpy as jnp
from jax import lax
from jax.experimental import pallas as pl
from jax.experimental.pallas import tpu as pltpu
from jax.sharding import PartitionSpec as P

KP = 128
MESH = pl.DeviceIdType.MESH


def place():
    lon = lax.axis_index("lon")
    lat = lax.axis_index("lat")
    return lon // 8, lon % 8, lat // 4, (lat // 2) % 2, lat % 2


def target(x, z_lo, y, z_hi, core):
    return {"lon": x * 8 + z_lo, "lat": y * 4 + z_hi * 2 + core}


def split(a):
    high = a.astype(jnp.bfloat16)
    return high, (a - high.astype(jnp.float32)).astype(jnp.bfloat16)


def product3(a, b, dims=(((1,), (0,)), ((), ()))):
    ah, al = split(a)
    bh, bl = split(b)
    dot = functools.partial(lax.dot_general, dimension_numbers=dims, preferred_element_type=jnp.float32)
    return dot(ah, bh) + (dot(ah, bl) + dot(al, bh))


def rise(t):
    series = 1.0 / 5040.0
    for c in (-1.0 / 720.0, 1.0 / 120.0, -1.0 / 24.0, 1.0 / 6.0, -0.5, 1.0):
        series = series * t + c
    return jnp.where(t < 0.25, t * series, 1.0 - jnp.exp(-t))


def lanes():
    return lax.broadcasted_iota(jnp.int32, (8, KP), 1)


def subs():
    return lax.broadcasted_iota(jnp.int32, (8, KP), 0)


def grouped(param_ref, kind, v, g):
    inv = 1.0 / param_ref[2 * kind, v, g]
    return inv, param_ref[2 * kind + 1, v, g] * (1.0 - jnp.exp(-inv))


def lat_gain(inv, coef, inv_all, coef_all, left):
    total = 0.0
    for q in range(4):
        both = inv + inv_all[q:q + 1]
        total = total + coef_all[q:q + 1] * (rise(both * left) / rise(both))
    return coef * total


def lat_tables(left_end, param_ref, take_ref, step_ref):
    j = (lanes() % 8).astype(jnp.float32)
    for v in range(2):
        for g in range(4):
            inv, coef = grouped(param_ref, 1, v, g)
            take_ref[v, g, 0] = jnp.exp(-(7.0 - j) * inv)
            take_ref[v, g, 1] = jnp.exp(-j * inv) * lat_gain(inv, coef, inv, coef, left_end - j)
            step_ref[v, g] = jnp.exp(-8.0 * inv)


def lane_tables(left_end, row_ref, param_ref, edge_ref, inv8_ref, closing_ref, lane_step_ref, lane_take_ref, gain_ref, nlon):
    low = subs() < 4
    cell = lanes().astype(jnp.float32)
    row = subs().astype(jnp.float32)
    for v in range(2):
        inv8 = jnp.zeros((8, KP), jnp.float32)
        inv_k = jnp.zeros((8, KP), jnp.float32)
        coef_k = jnp.zeros((8, KP), jnp.float32)
        for g in range(4):
            inv, coef = grouped(param_ref, 1, v, g)
            inv_k = jnp.where(row_ref[...] == g, inv, inv_k)
            coef_k = jnp.where(row_ref[...] == g, coef, coef_k)
            inv, _ = grouped(param_ref, 0, v, g)
            edge_ref[v, 8 * g:8 * g + 8] = jnp.exp(-jnp.where(low, 127.0 - cell, cell) * inv)
            inv8 = jnp.where(row_ref[...] == g, inv, inv8)
        inv8_ref[v] = inv8
        closing_ref[v] = 1.0 / rise(nlon * inv8)
        for p in range(4):
            inv, coef = inv_k[p:p + 1], coef_k[p:p + 1]
            gain = lat_gain(inv, coef, inv_k, coef_k, left_end - row)
            gain_ref[v, p] = gain
            lane_step_ref[v, p] = jnp.broadcast_to(jnp.exp(-8.0 * inv), (8, KP))
            lane_take_ref[v, p] = jnp.exp(-(7.0 - row) * inv)
            lane_take_ref[v, 4 + p] = jnp.exp(-row * inv) * gain
        gain_ref[v, 4] = inv_k


def late_tables(left_end, param_ref, gain_ref, inside_ref, decay_ref, apply_ref, local_ref, give_ref):
    low = subs() < 4
    cell = lanes().astype(jnp.float32)
    row = subs().astype(jnp.float32)
    j = (lanes() % 8).astype(jnp.float32)
    part = lanes() % 4
    for v in range(2):
        for g in range(4):
            inv, coef = grouped(param_ref, 0, v, g)
            amp = 0.0
            for q in range(4):
                amp = amp + coef[q:q + 1] / rise(inv + inv[q:q + 1])
            amp = coef * amp
            decay_ref[v, 8 * g:8 * g + 8] = amp * jnp.exp(-jnp.where(low, cell + 1.0, 128.0 - cell) * inv)
            for tile in range(16):
                gap = jnp.abs(row + 8.0 * tile - cell)
                total = 0.0
                for p in range(4):
                    total = total + amp[p:p + 1] * jnp.exp(-gap * inv[p:p + 1])
                inside_ref[v, 8 * tile:8 * tile + 8, KP * g:KP * g + KP] = total
            inv, coef = grouped(param_ref, 1, v, g)
            total = 0.0
            by_lane, coef_lane = jnp.zeros((8, KP), jnp.float32), jnp.zeros((8, KP), jnp.float32)
            for p in range(4):
                gain = lat_gain(inv[p:p + 1], coef[p:p + 1], inv, coef, left_end - jnp.maximum(row, j))
                total = total + gain * jnp.exp(-jnp.abs(row - j) * inv[p:p + 1])
                by_lane = jnp.where(part == p, inv[p:p + 1], by_lane)
                coef_lane = jnp.where(part == p, coef[p:p + 1], coef_lane)
            apply_ref[v, g, :, 0:KP] = total
            gain = lat_gain(by_lane, coef_lane, inv, coef, left_end - row)
            apply_ref[v, g, :, KP:2 * KP] = jnp.where(lanes() < 64, gain * jnp.exp(-(row + 1.0) * by_lane), jnp.exp(-(8.0 - row) * by_lane))
        inv_k = gain_ref[v, 4]
        for p in range(4):
            give_ref[v, p] = gain_ref[v, p] * jnp.exp(-(row + 1.0) * inv_k[p:p + 1])
            give_ref[v, 4 + p] = jnp.exp(-(8.0 - row) * inv_k[p:p + 1])
        for i in range(8):
            total = 0.0
            for p in range(4):
                gain = jnp.where(row >= i, gain_ref[v, p], gain_ref[v, p, i:i + 1])
                total = total + gain * jnp.exp(-jnp.abs(row - i) * inv_k[p:p + 1])
            local_ref[v, i] = total


def filter_kernel(nlat, nlon, raw_group_ref, raw_row_ref, lon_reach_ref, lon_weight_ref, lat_reach_ref, lat_weight_ref, raw_vertical_ref,
                    inc_ref, std_ref, out_ref, row_ref, param_ref, vertical_ref,
                    w_ref, wu_ref, u_ref, inside_ref, decay_ref, apply_ref, local_ref, give_ref, level_ref, both_ref, y_ref, carry_ref, uz_ref,
                    m_ref, me_ref, r8_ref, x_ref, bd_ref, take_pat_ref, step_pat_ref, edge_ref, inv_ref, closing_ref, step_ref, take_ref, gain_ref,
                    d1_ref, pm_ref, zr_ref, q_ref, yr_ref, ws_ref,
                    ud1_ref, um_ref, upm_ref, uzr_ref, uq_ref, uyr_ref, uws_ref,
                    rows_ref, total_ref, xr_ref, back_ref,
                    d1s, d1r, zss, zrs, yss, yrs, d2s, d2r, ls, lr, xs, xrs, bs, br):
    x, z_lo, y, z_hi, core = place()
    chunks = m_ref.shape[1]
    mate = target(x, z_lo, y, z_hi, 1 - core)
    across = target(x, z_lo, y, 1 - z_hi, core)
    ys = [target(x, z_lo, (y + d) % 4, z_hi, core) for d in (1, 2, 3)]
    xs_to = [target((x + d) % 4, z_lo, y, z_hi, core) for d in (1, 2, 3)]
    others = [target(x, (z_lo + d) % 8, y, z_hi, core) for d in range(1, 8)]
    partners = [mate, across] + ys + xs_to + others
    barrier = pltpu.get_barrier_semaphore()
    for p in partners:
        pl.semaphore_signal(barrier, inc=1, device_id=p, device_id_type=MESH)
    levels = inc_ref.shape[1]
    row_ref[:, 0:levels] = raw_row_ref[...]
    row_ref[:, levels:KP] = jnp.broadcast_to(raw_row_ref[:, levels - 1:levels], (1, KP - levels))
    part = subs() % 4
    for kind, ref in enumerate((lon_reach_ref, lon_weight_ref, lat_reach_ref, lat_weight_ref)):
        for v in range(2):
            for g in range(4):
                tile = jnp.full((8, KP), ref[v, g, 0])
                for p in range(1, 4):
                    tile = jnp.where(part == p, ref[v, g, p], tile)
                param_ref[kind, v, g] = tile

    def group_of(k):
        return raw_group_ref[jnp.minimum(k, levels - 1)]

    left_end = (nlat - 8 * lax.axis_index("lat")).astype(jnp.float32)
    lat_tables(left_end, param_ref, take_pat_ref, step_pat_ref)
    for v in range(2):
        product = inc_ref[v].astype(jnp.float32) * std_ref[v].astype(jnp.float32)
        x_ref[v, pl.ds(0, levels * 8)] = product.reshape(levels * 8, KP)
        x_ref[v, pl.ds(levels * 8, 8 * (KP - levels))] = jnp.zeros((8 * (KP - levels), KP), jnp.float32)

    def build(t, carry):
        g0, g1 = group_of(2 * t), group_of(2 * t + 1)
        block, sub = t // 8, t % 8
        low = subs() < 4
        own = jnp.where(low, 2 * sub, 2 * sub + 1) == lanes() // 8
        for v in range(2):
            r8_ref[v, block, sub] = jnp.where(low, step_pat_ref[v, g0], step_pat_ref[v, g1])
            for part in range(2):
                tile = jnp.where(own, jnp.where(low, take_pat_ref[v, g0, part], take_pat_ref[v, g1, part]), 0.0)
                bd_ref[v, block, pl.ds(pl.multiple_of(part * 64 + sub * 8, 8), 8)] = tile
        return carry

    def moments(c):
        v = c // 4
        for half in range(2):
            block = half * 4 + c % 4
            out = product3(bd_ref[v, block], x_ref[v, pl.ds(block * 128, 128)])
            m_ref[half, c] = out.reshape(2, 8, 8, KP)

    def lon_sums():
        lane_tables(left_end, row_ref, param_ref, edge_ref, inv_ref, closing_ref, step_ref, take_ref, gain_ref, float(nlon))
        for v in range(2):
            for i in range(8):
                sums = product3(edge_ref[v], x_ref[v, pl.ds(i, KP, stride=8)], (((1,), (1,)), ((), ())))
                me_ref[i, v] = functools.reduce(jnp.add, [jnp.where(row_ref[...] == g, sums[8 * g:8 * g + 8], 0.0) for g in range(4)])
    def late():
        late_tables(left_end, param_ref, gain_ref, inside_ref, decay_ref, apply_ref, local_ref, give_ref)

        vertical_ref[...] = jnp.zeros_like(vertical_ref)
        vertical_ref[:, 0:levels, 0:levels] = raw_vertical_ref[...]

        def place_level(k, carry):
            g = group_of(k)
            lane = lax.broadcasted_iota(jnp.int32, (8, 2 * KP), 1)
            own = jnp.where(lane < KP, lane // 8, (lane % 64) // 4) == k % 16
            rows = pl.ds(pl.multiple_of(k * 8, 8), 8)
            level_ref[rows] = jnp.full((8, KP), g, jnp.int32)
            for v in range(2):
                both_ref[v, rows] = jnp.where(own, apply_ref[v, g], 0.0)
            return carry

        lax.fori_loop(0, KP, place_level, 0)

    def stage_f(c):
        v = c // 4
        d2(c).wait_recv()
        for half in range(2):
            block = half * 4 + c % 4
            rows = pl.ds(block * 128, 128)
            source = jnp.concatenate([x_ref[v, rows], w_ref[half, c].reshape(128, KP)], axis=0)
            z = product3(both_ref[v, rows], source)
            wide = product3(z, inside_ref[v])
            result = wide[:, 0:KP]
            for g in range(1, 4):
                result = jnp.where(level_ref[rows] == g, wide[:, KP * g:KP * g + KP], result)
            y_ref[v, rows] = result

    def carried():
        ud2.wait_recv()
        for v in range(2):
            for i in range(8):
                acc = local_ref[v, i, 0:1] * u_ref[0, v]
                for j in range(1, 8):
                    acc = acc + local_ref[v, i, j:j + 1] * u_ref[j, v]
                for m in range(8):
                    acc = acc + give_ref[v, m, i:i + 1] * wu_ref[v, m // 4, m % 4]
                for g in range(4):
                    uz_ref[8 * g:8 * g + 8] = jnp.where(row_ref[...] == g, acc, 0.0)
                carry_ref[v, i] = product3(uz_ref[...], decay_ref[v], (((0,), (0,)), ((), ())))

    def mix(v):
        for i in range(8):
            rows = pl.ds(i, KP, stride=8)
            x_ref[v, rows] = product3(vertical_ref[v], y_ref[v, rows] + carry_ref[v, i])
        mixed = x_ref[v, pl.ds(0, levels * 8)].reshape(levels, 8, KP)
        out_ref[v] = (std_ref[v].astype(jnp.float32) * mixed).astype(jnp.bfloat16)

    lax.fori_loop(0, KP // 2, build, 0)
    moments(0)
    lon_sums()
    moments(1)
    pl.semaphore_wait(barrier, len(partners))

    def remote(src, dst, s, r, to):
        return pltpu.make_async_remote_copy(src_ref=src, dst_ref=dst, send_sem=s, recv_sem=r, device_id=to, device_id_type=MESH)

    def d1(c):
        return remote(m_ref.at[1 - core, c], d1_ref.at[c], d1s.at[c], d1r.at[c], mate)

    def zc(c):
        return remote(pm_ref.at[c], zr_ref.at[c], zss.at[c], zrs.at[c], across)

    def yc(c, d):
        part = (y + d) // 4
        return remote(q_ref.at[c, part], yr_ref.at[c, d - 1], yss.at[c, d - 1], yrs.at[c, d - 1], ys[d - 1])

    def d2(c):
        return remote(ws_ref.at[c], w_ref.at[core, c], d2s.at[c], d2r.at[c], mate)

    last = chunks
    ud1 = remote(um_ref.at[1 - core], ud1_ref, d1s.at[last], d1r.at[last], mate)
    uz = remote(upm_ref, uzr_ref, zss.at[last], zrs.at[last], across)
    uy = [remote(uq_ref.at[(y + d) // 4], uyr_ref.at[d - 1], yss.at[last, d - 1], yrs.at[last, d - 1], ys[d - 1]) for d in (1, 2, 3)]
    ud2 = remote(uws_ref, wu_ref.at[core], d2s.at[last], d2r.at[last], mate)

    def weigh(first, r, own, other):
        a = jnp.where(first, r, 1.0)
        b = jnp.where(first, 1.0, r)
        return a * own[0] + b * other[0], b * own[1] + a * other[1]

    def finish(r8, own, part, zr, slots):
        r16 = r8 * r8
        r32 = r16 * r16
        powers = [jnp.ones_like(r32), r32, r32 * r32]
        wf = jnp.zeros_like(r8)
        wb = jnp.zeros_like(r8)
        for d in (1, 2, 3):
            before = y >= d
            wf = wf + jnp.where(before, powers[d - 1] * slots[d - 1], 0.0)
            wb = wb + jnp.where(before, 0.0, powers[3 - d] * slots[d - 1])
        lower = z_hi == 0
        wf, wb = jnp.where(lower, wf, r16 * wf + zr[0]), jnp.where(lower, r16 * wb + zr[1], wb)
        first = core == 0
        far_f, far_b = r8 * wf, r8 * wb
        mine = jnp.where(first, wf, far_f + part[0]), jnp.where(first, far_b + part[1], wb)
        theirs = jnp.where(first, far_f + own[0], wf), jnp.where(first, wb, far_b + own[1])
        return mine, theirs

    def rate(c):
        return r8_ref[c // 4, core * 4 + c % 4]

    def stage_z(c):
        d1(c).wait_recv()
        f, b = weigh(core == 0, rate(c), (m_ref[core, c, 0], m_ref[core, c, 1]), (d1_ref[c, 0], d1_ref[c, 1]))
        pm_ref[c, 0] = f
        pm_ref[c, 1] = b
        zc(c).start()

    def stage_y(c):
        zc(c).wait_recv()
        r8 = rate(c)
        f, b = weigh(z_hi == 0, r8 * r8, (pm_ref[c, 0], pm_ref[c, 1]), (zr_ref[c, 0], zr_ref[c, 1]))
        q_ref[c, 0] = f
        q_ref[c, 1] = b
        for d in (1, 2, 3):
            yc(c, d).start()

    def stage_w(c):
        for d in (1, 2, 3):
            yc(c, d).wait_recv()
        mine, theirs = finish(rate(c), (m_ref[core, c, 0], m_ref[core, c, 1]), (d1_ref[c, 0], d1_ref[c, 1]),
                              (zr_ref[c, 0], zr_ref[c, 1]), [yr_ref[c, d] for d in range(3)])
        w_ref[core, c, 0] = mine[0]
        w_ref[core, c, 1] = mine[1]
        ws_ref[c, 0] = theirs[0]
        ws_ref[c, 1] = theirs[1]
        d2(c).start()

    is_f = lax.broadcasted_iota(jnp.int32, (1, 8, KP), 1) < 4
    gather = [remote(me_ref.at[(z_lo + d) % 8], rows_ref.at[z_lo], ls.at[d - 1], lr.at[d - 1], others[d - 1]) for d in range(1, 8)]
    spread = [remote(back_ref.at[(z_lo + d) % 8], u_ref.at[z_lo], bs.at[d - 1], br.at[d - 1], others[d - 1]) for d in range(1, 8)]
    xcopies = [remote(total_ref, xr_ref.at[d], xs.at[d], xrs.at[d], xs_to[d]) for d in range(3)]

    def lon_totals():
        rows_ref[z_lo] = me_ref[z_lo]
        for cp in gather:
            cp.wait_recv()
        step = jnp.exp(-128.0 * inv_ref[...])
        total = jnp.zeros_like(step)
        for k in range(8):
            total = step * total + jnp.where(is_f, rows_ref[k], rows_ref[7 - k])
        total_ref[...] = total
        for cp in xcopies:
            cp.start()

    def lon_states():
        for cp in xcopies:
            cp.wait_recv()
        inv = inv_ref[...]
        step = jnp.exp(-128.0 * inv)
        r1 = jnp.exp(-1024.0 * inv)
        powers = [jnp.ones_like(r1), r1, r1 * r1]
        state = powers[2] * r1 * total_ref[...]
        for d in range(3):
            state = state + jnp.where(is_f, powers[d], powers[2 - d]) * xr_ref[d]
        states = [closing_ref[...] * state]
        for k in range(7):
            states.append(step * states[-1] + jnp.where(is_f, rows_ref[k], rows_ref[7 - k]))
        for k in range(8):
            back_ref[k] = jnp.where(is_f, states[k], states[7 - k])
        u_ref[z_lo] = back_ref[z_lo]
        for cp in spread:
            cp.start()

    def lon_moments():
        for cp in spread:
            cp.wait_recv()
        for v in range(2):
            for m in range(8):
                acc = take_ref[v, m, 0:1] * u_ref[0, v]
                for j in range(1, 8):
                    acc = acc + take_ref[v, m, j:j + 1] * u_ref[j, v]
                um_ref[v, m // 4, m % 4] = acc
        ud1.start()

    def small_own():
        return step_ref[core], (um_ref[core, 0], um_ref[core, 1]), (ud1_ref[0], ud1_ref[1])

    def small_z():
        ud1.wait_recv()
        r8, own, part = small_own()
        f, b = weigh(core == 0, r8, own, part)
        upm_ref[0] = f
        upm_ref[1] = b
        uz.start()

    def small_y():
        uz.wait_recv()
        r8 = step_ref[core]
        f, b = weigh(z_hi == 0, r8 * r8, (upm_ref[0], upm_ref[1]), (uzr_ref[0], uzr_ref[1]))
        uq_ref[0] = f
        uq_ref[1] = b
        for cp in uy:
            cp.start()

    def small_w():
        for cp in uy:
            cp.wait_recv()
        r8, own, part = small_own()
        mine, theirs = finish(r8, own, part, (uzr_ref[0], uzr_ref[1]), [uyr_ref[d] for d in range(3)])
        wu_ref[core, 0] = mine[0]
        wu_ref[core, 1] = mine[1]
        uws_ref[0] = theirs[0]
        uws_ref[1] = theirs[1]
        ud2.start()

    def early(c):
        if c > 1:
            moments(c)
        d1(c).start()

    for cp in gather:
        cp.start()
    early(0)
    early(1)
    stage_z(0)
    early(2)
    stage_z(1)
    early(3)
    stage_z(2)
    lon_totals()
    early(4)
    early(5)
    lon_states()
    early(6)
    early(7)
    late()
    stage_y(0)
    stage_z(3)
    stage_y(1)
    stage_z(4)
    stage_w(0)
    stage_f(0)
    stage_y(2)
    stage_z(5)
    stage_w(1)
    stage_y(3)
    stage_z(6)
    stage_w(2)
    stage_f(1)
    lon_moments()
    stage_y(4)
    stage_z(7)
    stage_w(3)
    stage_f(2)
    small_z()
    stage_y(5)
    stage_w(4)
    stage_f(3)
    stage_y(6)
    small_y()
    stage_w(5)
    stage_f(4)
    stage_y(7)
    small_w()
    stage_w(6)
    stage_f(5)
    carried()
    mix(0)
    stage_w(7)
    stage_f(6)
    stage_f(7)
    mix(1)

    def drain(c, carry):
        d1(c).wait_send()
        zc(c).wait_send()
        for d in (1, 2, 3):
            yc(c, d).wait_send()
        d2(c).wait_send()
        return carry

    lax.fori_loop(0, chunks, drain, 0)
    for cp in gather + xcopies + spread + [ud1, uz] + uy:
        cp.wait_send()
    ud2.wait_send()


def per_device(nlat, nlon, increment, std_dev, level_group, lon_reach, lon_weight, lat_reach, lat_weight, vertical):
    vs, levels, rows, cells = increment.shape
    f32 = jnp.float32
    vmem = pl.BlockSpec(memory_space=pltpu.VMEM)
    smem = pl.BlockSpec(memory_space=pltpu.SMEM)
    limit = 48 << 20

    dma = pltpu.SemaphoreType.DMA
    chunk = (2, 8, 8, KP)
    small = (2, 4, 8, KP)

    def scratch(*dims):
        return pltpu.VMEM(dims, f32)

    return pl.pallas_call(
        functools.partial(filter_kernel, nlat, nlon),
        out_shape=jax.ShapeDtypeStruct(increment.shape, jnp.bfloat16),
        in_specs=[smem, vmem] + [smem] * 4 + [vmem] * 3,
        out_specs=vmem,
        scratch_shapes=[
            pltpu.VMEM((1, KP), jnp.int32), scratch(4, vs, 4, 8, KP), scratch(vs, KP, KP),
            scratch(2, 8, *chunk), scratch(vs, *small), scratch(8, vs, 8, KP), scratch(vs, KP, 4 * KP), scratch(vs, 32, KP),
            scratch(vs, 4, 8, 2 * KP), scratch(vs, 8, 8, KP), scratch(vs, 8, 8, KP), pltpu.VMEM((8 * KP, KP), jnp.int32),
            scratch(vs, 8 * KP, 2 * KP), scratch(vs, 8 * KP, KP), scratch(vs, 8, KP, KP), scratch(32, KP),
            scratch(2, 8, *chunk), scratch(8, vs, 8, KP), scratch(vs, 8, 8, 8, KP), scratch(vs, 8 * KP, KP), scratch(vs, 8, 128, KP),
            scratch(vs, 4, 2, 8, KP), scratch(vs, 4, 8, KP), scratch(vs, 32, KP), scratch(vs, 8, KP), scratch(vs, 8, KP), scratch(vs, 4, 8, KP),
            scratch(vs, 8, 8, KP), scratch(vs, 5, 8, KP),
            scratch(8, *chunk), scratch(8, *chunk), scratch(8, *chunk), scratch(8, *chunk), scratch(8, 3, *chunk[1:]), scratch(8, *chunk),
            scratch(*small), scratch(vs, *small), scratch(*small), scratch(*small), scratch(*small), scratch(3, *small[1:]), scratch(*small),
            scratch(8, vs, 8, KP), scratch(vs, 8, KP), scratch(3, vs, 8, KP), scratch(8, vs, 8, KP),
            dma((9,)), dma((9,)), dma((9,)), dma((9,)), dma((9, 3)), dma((9, 3)), dma((9,)), dma((9,)),
            dma((7,)), dma((7,)), dma((3,)), dma((3,)), dma((7,)), dma((7,)),
        ],
        compiler_params=pltpu.CompilerParams(collective_id=0, has_side_effects=True, vmem_limit_bytes=limit),
        name="filter",
    )(level_group, level_group[None, :], lon_reach, lon_weight, lat_reach, lat_weight, vertical, increment, std_dev)


def solution(mesh):
    placed = (P(None, None, "lat", "lon"),) * 2 + (P(),) * 6

    def whole(increment, *rest):
        nlat, nlon = increment.shape[2:]
        body = functools.partial(per_device, nlat, nlon)
        return jax.shard_map(body, mesh=mesh, in_specs=placed, out_specs=P(None, None, "lat", "lon"), check_vma=False)(increment, *rest)

    return whole
```

```python
import functools

import jax
import jax.numpy as jnp
from jax import lax
from jax.experimental import pallas as pl
from jax.experimental.pallas import tpu as pltpu
from jax.sharding import PartitionSpec as P

KP = 128
MESH = pl.DeviceIdType.MESH


def place():
    lon = lax.axis_index("lon")
    lat = lax.axis_index("lat")
    return lon // 8, lon % 8, lat // 4, (lat // 2) % 2, lat % 2


def target(x, z_lo, y, z_hi, core):
    return {"lon": x * 8 + z_lo, "lat": y * 4 + z_hi * 2 + core}


def split(a):
    high = a.astype(jnp.bfloat16)
    return high, (a - high.astype(jnp.float32)).astype(jnp.bfloat16)


def product3(a, b, dims=(((1,), (0,)), ((), ()))):
    ah, al = split(a)
    bh, bl = split(b)
    dot = functools.partial(lax.dot_general, dimension_numbers=dims, preferred_element_type=jnp.float32)
    return dot(ah, bh) + (dot(ah, bl) + dot(al, bh))


def rise(t):
    series = 1.0 / 5040.0
    for c in (-1.0 / 720.0, 1.0 / 120.0, -1.0 / 24.0, 1.0 / 6.0, -0.5, 1.0):
        series = series * t + c
    return jnp.where(t < 0.25, t * series, 1.0 - jnp.exp(-t))


def lanes():
    return lax.broadcasted_iota(jnp.int32, (8, KP), 1)


def subs():
    return lax.broadcasted_iota(jnp.int32, (8, KP), 0)


def grouped(param_ref, kind, v, g):
    inv = 1.0 / param_ref[2 * kind, v, g]
    return inv, param_ref[2 * kind + 1, v, g] * (1.0 - jnp.exp(-inv))


def lat_gain(inv, coef, inv_all, coef_all, left):
    total = 0.0
    for q in range(4):
        both = inv + inv_all[q:q + 1]
        total = total + coef_all[q:q + 1] * (rise(both * left) / rise(both))
    return coef * total


def lat_tables(left_end, param_ref, take_ref, step_ref):
    j = (lanes() % 8).astype(jnp.float32)
    for v in range(2):
        for g in range(4):
            inv, coef = grouped(param_ref, 1, v, g)
            take_ref[v, g, 0] = jnp.exp(-(7.0 - j) * inv)
            take_ref[v, g, 1] = jnp.exp(-j * inv) * lat_gain(inv, coef, inv, coef, left_end - j)
            step_ref[v, g] = jnp.exp(-8.0 * inv)


def lane_tables(left_end, row_ref, param_ref, edge_ref, inv8_ref, closing_ref, lane_step_ref, lane_take_ref, gain_ref, nlon):
    low = subs() < 4
    cell = lanes().astype(jnp.float32)
    row = subs().astype(jnp.float32)
    for v in range(2):
        inv8 = jnp.zeros((8, KP), jnp.float32)
        inv_k = jnp.zeros((8, KP), jnp.float32)
        coef_k = jnp.zeros((8, KP), jnp.float32)
        for g in range(4):
            inv, coef = grouped(param_ref, 1, v, g)
            inv_k = jnp.where(row_ref[...] == g, inv, inv_k)
            coef_k = jnp.where(row_ref[...] == g, coef, coef_k)
            inv, _ = grouped(param_ref, 0, v, g)
            edge_ref[v, 8 * g:8 * g + 8] = jnp.exp(-jnp.where(low, 127.0 - cell, cell) * inv)
            inv8 = jnp.where(row_ref[...] == g, inv, inv8)
        inv8_ref[v] = inv8
        closing_ref[v] = 1.0 / rise(nlon * inv8)
        for p in range(4):
            inv, coef = inv_k[p:p + 1], coef_k[p:p + 1]
            gain = lat_gain(inv, coef, inv_k, coef_k, left_end - row)
            gain_ref[v, p] = gain
            lane_step_ref[v, p] = jnp.broadcast_to(jnp.exp(-8.0 * inv), (8, KP))
            lane_take_ref[v, p] = jnp.exp(-(7.0 - row) * inv)
            lane_take_ref[v, 4 + p] = jnp.exp(-row * inv) * gain
        gain_ref[v, 4] = inv_k


def late_tables(left_end, param_ref, gain_ref, inside_ref, decay_ref, apply_ref, local_ref, give_ref):
    low = subs() < 4
    cell = lanes().astype(jnp.float32)
    row = subs().astype(jnp.float32)
    j = (lanes() % 8).astype(jnp.float32)
    part = lanes() % 64 // 16
    for v in range(2):
        for g in range(4):
            inv, coef = grouped(param_ref, 0, v, g)
            amp = 0.0
            for q in range(4):
                amp = amp + coef[q:q + 1] / rise(inv + inv[q:q + 1])
            amp = coef * amp
            decay_ref[v, 8 * g:8 * g + 8] = amp * jnp.exp(-jnp.where(low, cell + 1.0, 128.0 - cell) * inv)
            for tile in range(16):
                gap = jnp.abs(row + 8.0 * tile - cell)
                total = 0.0
                for p in range(4):
                    total = total + amp[p:p + 1] * jnp.exp(-gap * inv[p:p + 1])
                inside_ref[v, 8 * tile:8 * tile + 8, KP * g:KP * g + KP] = total
            inv, coef = grouped(param_ref, 1, v, g)
            total = 0.0
            by_lane, coef_lane = jnp.zeros((8, KP), jnp.float32), jnp.zeros((8, KP), jnp.float32)
            for p in range(4):
                gain = lat_gain(inv[p:p + 1], coef[p:p + 1], inv, coef, left_end - jnp.maximum(row, j))
                total = total + gain * jnp.exp(-jnp.abs(row - j) * inv[p:p + 1])
                by_lane = jnp.where(part == p, inv[p:p + 1], by_lane)
                coef_lane = jnp.where(part == p, coef[p:p + 1], coef_lane)
            apply_ref[v, g, :, 0:KP] = total
            gain = lat_gain(by_lane, coef_lane, inv, coef, left_end - row)
            apply_ref[v, g, :, KP:2 * KP] = jnp.where(lanes() < 64, gain * jnp.exp(-(row + 1.0) * by_lane), jnp.exp(-(8.0 - row) * by_lane))
        inv_k = gain_ref[v, 4]
        for p in range(4):
            give_ref[v, p] = gain_ref[v, p] * jnp.exp(-(row + 1.0) * inv_k[p:p + 1])
            give_ref[v, 4 + p] = jnp.exp(-(8.0 - row) * inv_k[p:p + 1])
        for i in range(8):
            total = 0.0
            for p in range(4):
                gain = jnp.where(row >= i, gain_ref[v, p], gain_ref[v, p, i:i + 1])
                total = total + gain * jnp.exp(-jnp.abs(row - i) * inv_k[p:p + 1])
            local_ref[v, i] = total


def filter_kernel(nlat, nlon, raw_group_ref, raw_row_ref, lon_reach_ref, lon_weight_ref, lat_reach_ref, lat_weight_ref, raw_vertical_ref,
                    inc_ref, std_ref, out_ref, row_ref, param_ref, vertical_ref,
                    w_ref, wu_ref, u_ref, inside_ref, decay_ref, apply_ref, local_ref, give_ref, level_ref, both_ref, y_ref, carry_ref, uz_ref,
                    m_ref, me_ref, r8_ref, x_ref, bd_ref, take_pat_ref, step_pat_ref, edge_ref, inv_ref, closing_ref, step_ref, take_ref, gain_ref,
                    d1_ref, pm_ref, zr_ref, q_ref, yr_ref, ws_ref,
                    ud1_ref, um_ref, upm_ref, uzr_ref, uq_ref, uyr_ref, uws_ref,
                    rows_ref, total_ref, xr_ref, back_ref, zo_ref, un_ref, fo_ref, fi_ref,
                    d1s, d1r, zss, zrs, yss, yrs, d2s, d2r, ls, lr, xs, xrs, bs, br, uns, unr, fos, fir):
    x, z_lo, y, z_hi, core = place()
    chunks = m_ref.shape[1]
    mate = target(x, z_lo, y, z_hi, 1 - core)
    across = target(x, z_lo, y, 1 - z_hi, core)
    ys = [target(x, z_lo, (y + d) % 4, z_hi, core) for d in (1, 2, 3)]
    xs_to = [target((x + d) % 4, z_lo, y, z_hi, core) for d in (1, 2, 3)]
    others = [target(x, (z_lo + d) % 8, y, z_hi, core) for d in range(1, 8)]
    partners = [mate, across] + ys + xs_to + others
    barrier = pltpu.get_barrier_semaphore()
    for p in partners:
        pl.semaphore_signal(barrier, inc=1, device_id=p, device_id_type=MESH)
    levels = inc_ref.shape[1]
    row_ref[:, 0:levels] = raw_row_ref[...]
    row_ref[:, levels:KP] = jnp.broadcast_to(raw_row_ref[:, levels - 1:levels], (1, KP - levels))
    part = subs() % 4
    for kind, ref in enumerate((lon_reach_ref, lon_weight_ref, lat_reach_ref, lat_weight_ref)):
        for v in range(2):
            for g in range(4):
                tile = jnp.full((8, KP), ref[v, g, 0])
                for p in range(1, 4):
                    tile = jnp.where(part == p, ref[v, g, p], tile)
                param_ref[kind, v, g] = tile

    def group_of(k):
        return raw_group_ref[jnp.minimum(k, levels - 1)]

    left_end = (nlat - 8 * lax.axis_index("lat")).astype(jnp.float32)
    lat_tables(left_end, param_ref, take_pat_ref, step_pat_ref)
    for v in range(2):
        product = inc_ref[v].astype(jnp.float32) * std_ref[v].astype(jnp.float32)
        x_ref[v, pl.ds(0, levels * 8)] = product.reshape(levels * 8, KP)
        x_ref[v, pl.ds(levels * 8, 8 * (KP - levels))] = jnp.zeros((8 * (KP - levels), KP), jnp.float32)

    starts = [jnp.sum((row_ref[...] < g).astype(jnp.int32)) for g in (1, 2, 3)]

    def build(t, carry):
        block, half = t // 2, t % 2
        level = 8 * t + subs()
        own = lanes() // 8 == 8 * half + subs()

        def choose(rows):
            tile = jnp.broadcast_to(rows[0], (8, KP))
            for g in range(1, 4):
                tile = jnp.where(level >= starts[g - 1], rows[g], tile)
            return tile

        for v in range(2):
            for p in range(4):
                r8_ref[v, block, 2 * p + half] = choose([step_pat_ref[v, g, p:p + 1] for g in range(4)])
                for part in range(2):
                    tile = choose([take_pat_ref[v, g, part, p:p + 1] for g in range(4)])
                    bd_ref[v, block, pl.ds(pl.multiple_of(part * 64 + p * 16 + half * 8, 8), 8)] = jnp.where(own, tile, 0.0)
        return carry

    def moments(c):
        v = c // 4
        for half in range(2):
            block = half * 4 + c % 4
            out = product3(bd_ref[v, block], x_ref[v, pl.ds(block * 128, 128)])
            m_ref[half, c] = out.reshape(2, 8, 8, KP)

    def lon_sums():
        lane_tables(left_end, row_ref, param_ref, edge_ref, inv_ref, closing_ref, step_ref, take_ref, gain_ref, float(nlon))
        for v in range(2):
            for i in range(8):
                sums = product3(edge_ref[v], x_ref[v, pl.ds(i, KP, stride=8)], (((1,), (1,)), ((), ())))
                me_ref[i, v] = functools.reduce(jnp.add, [jnp.where(row_ref[...] == g, sums[8 * g:8 * g + 8], 0.0) for g in range(4)])
    def late():
        late_tables(left_end, param_ref, gain_ref, inside_ref, decay_ref, apply_ref, local_ref, give_ref)

        vertical_ref[...] = jnp.zeros_like(vertical_ref)
        vertical_ref[:, 0:levels, 0:levels] = raw_vertical_ref[...]

        def place_level(k, carry):
            g = group_of(k)
            lane = lax.broadcasted_iota(jnp.int32, (8, 2 * KP), 1)
            own = jnp.where(lane < KP, lane // 8, lane % 16) == k % 16
            rows = pl.ds(pl.multiple_of(k * 8, 8), 8)
            level_ref[rows] = jnp.full((8, KP), g, jnp.int32)
            for v in range(2):
                both_ref[v, rows] = jnp.where(own, apply_ref[v, g], 0.0)
            return carry

        lax.fori_loop(0, KP, place_level, 0)

    def stage_f(c):
        v = c // 4
        d2(c).wait_recv()
        for half in range(2):
            block = half * 4 + c % 4
            rows = pl.ds(block * 128, 128)
            source = jnp.concatenate([x_ref[v, rows], w_ref[half, c].reshape(128, KP)], axis=0)
            z = product3(both_ref[v, rows], source)
            wide = product3(z, inside_ref[v])
            result = wide[:, 0:KP]
            for g in range(1, 4):
                result = jnp.where(level_ref[rows] == g, wide[:, KP * g:KP * g + KP], result)
            y_ref[v, rows] = result

    def carried():
        ud2.wait_recv()
        for v in range(2):
            for i in range(8):
                acc = local_ref[v, i, 0:1] * u_ref[0, v]
                for j in range(1, 8):
                    acc = acc + local_ref[v, i, j:j + 1] * u_ref[j, v]
                for m in range(8):
                    acc = acc + give_ref[v, m, i:i + 1] * wu_ref[v, m // 4, m % 4]
                for g in range(4):
                    uz_ref[8 * g:8 * g + 8] = jnp.where(row_ref[...] == g, acc, 0.0)
                carry_ref[v, i] = product3(uz_ref[...], decay_ref[v], (((0,), (0,)), ((), ())))

    def mix(v):
        for i in range(8):
            rows = pl.ds(i, KP, stride=8)
            x_ref[v, rows] = product3(vertical_ref[v], y_ref[v, rows] + carry_ref[v, i])
        mixed = x_ref[v, pl.ds(0, levels * 8)].reshape(levels, 8, KP)
        out_ref[v] = (std_ref[v].astype(jnp.float32) * mixed).astype(jnp.bfloat16)

    lax.fori_loop(0, KP // 8, build, 0)
    moments(0)
    lon_sums()
    moments(1)
    pl.semaphore_wait(barrier, len(partners))

    def remote(src, dst, s, r, to):
        return pltpu.make_async_remote_copy(src_ref=src, dst_ref=dst, send_sem=s, recv_sem=r, device_id=to, device_id_type=MESH)

    def d1(c):
        return remote(m_ref.at[1 - core, c], d1_ref.at[c], d1s.at[c], d1r.at[c], mate)

    def zc(c):
        return remote(zo_ref.at[c], zr_ref.at[c], zss.at[c], zrs.at[c], across)

    send_e = jnp.where(z_hi == 0, y, 3 - y)
    recv_e = jnp.where(z_hi == 1, y, 3 - y)
    send_hub = target(x, z_lo, 3 * z_hi, z_hi, core)
    recv_to = [target(x, z_lo, jnp.where(z_hi == 1, e, 3 - e), z_hi, core) for e in (1, 2)]

    def unit_out(c):
        e = jnp.maximum(send_e, 1)
        return remote(pm_ref.at[c, 1 - z_hi, pl.ds(6, 2)], un_ref.at[c, e - 1], uns.at[c], unr.at[c, e - 1], send_hub)

    def unit_in(c, k):
        return remote(pm_ref.at[c, 1 - z_hi, pl.ds(6, 2)], un_ref.at[c, k], uns.at[c], unr.at[c, k], across)

    def fix_out(c, k):
        return remote(fo_ref.at[c, k], fi_ref.at[c], fos.at[c, k], fir.at[c], recv_to[k])

    def fix_in(c):
        return remote(fo_ref.at[c, 0], fi_ref.at[c], fos.at[c, 0], fir.at[c], across)

    def yc(c, d):
        part = (y + d) // 4
        return remote(q_ref.at[c, part], yr_ref.at[c, d - 1], yss.at[c, d - 1], yrs.at[c, d - 1], ys[d - 1])

    def d2(c):
        return remote(ws_ref.at[c], w_ref.at[core, c], d2s.at[c], d2r.at[c], mate)

    last = chunks
    ud1 = remote(um_ref.at[1 - core], ud1_ref, d1s.at[last], d1r.at[last], mate)
    uz = remote(upm_ref, uzr_ref, zss.at[last], zrs.at[last], across)
    uy = [remote(uq_ref.at[(y + d) // 4], uyr_ref.at[d - 1], yss.at[last, d - 1], yrs.at[last, d - 1], ys[d - 1]) for d in (1, 2, 3)]
    ud2 = remote(uws_ref, wu_ref.at[core], d2s.at[last], d2r.at[last], mate)

    def weigh(first, r, own, other):
        a = jnp.where(first, r, 1.0)
        b = jnp.where(first, 1.0, r)
        return a * own[0] + b * other[0], b * own[1] + a * other[1]

    def finish(r8, own, part, zr, slots, fix=None):
        r16 = r8 * r8
        r32 = r16 * r16
        powers = [jnp.ones_like(r32), r32, r32 * r32]
        wf = jnp.zeros_like(r8)
        wb = jnp.zeros_like(r8)
        for d in (1, 2, 3):
            before = y >= d
            wf = wf + jnp.where(before, powers[d - 1] * slots[d - 1], 0.0)
            wb = wb + jnp.where(before, 0.0, powers[3 - d] * slots[d - 1])
        if fix is not None:
            whole = jnp.concatenate([jnp.zeros((6, 8, KP), jnp.float32), fix], axis=0)
            wf = wf + jnp.where(z_hi == 0, whole, 0.0)
            wb = wb + jnp.where(z_hi == 0, 0.0, whole)
        lower = z_hi == 0
        wf, wb = jnp.where(lower, wf, r16 * wf + zr[0]), jnp.where(lower, r16 * wb + zr[1], wb)
        first = core == 0
        far_f, far_b = r8 * wf, r8 * wb
        mine = jnp.where(first, wf, far_f + part[0]), jnp.where(first, far_b + part[1], wb)
        theirs = jnp.where(first, far_f + own[0], wf), jnp.where(first, wb, far_b + own[1])
        return mine, theirs

    def rate(c):
        return r8_ref[c // 4, core * 4 + c % 4]

    def stage_p(c):
        d1(c).wait_recv()
        f, b = weigh(core == 0, rate(c), (m_ref[core, c, 0], m_ref[core, c, 1]), (d1_ref[c, 0], d1_ref[c, 1]))
        pm_ref[c, 0] = f
        pm_ref[c, 1] = b
        zo_ref[c, 0:8] = jnp.where(z_hi == 0, f, b)
        zo_ref[c, 8:14] = jnp.where(z_hi == 0, b, f)[0:6]

        @pl.when(send_e > 0)
        def _():
            unit_out(c).start()

    def stage_z(c):
        @pl.when(send_e == 0)
        def _():
            for k in range(3):
                unit_in(c, k).wait_recv()
                zo_ref[c, 8 + 2 * k:10 + 2 * k] = un_ref[c, k]

        zc(c).start()

    def across_parts(c):
        kept = zr_ref[c, 0:8]
        rest = jnp.concatenate([zr_ref[c, 8:14], jnp.zeros((2, 8, KP), jnp.float32)], axis=0)
        return jnp.where(z_hi == 1, kept, rest), jnp.where(z_hi == 1, rest, kept)

    def stage_y(c):
        zc(c).wait_recv()
        r8 = rate(c)
        f, b = weigh(z_hi == 0, r8 * r8, (pm_ref[c, 0], pm_ref[c, 1]), across_parts(c))
        q_ref[c, 0] = f
        q_ref[c, 1] = b
        for d in (1, 2, 3):
            yc(c, d).start()

        @pl.when(recv_e == 0)
        def _():
            r32 = r8[6:8] * r8[6:8]
            r32 = r32 * r32
            third = zr_ref[c, 12:14]
            second = zr_ref[c, 10:12] + r32 * third
            fo_ref[c, 1] = third
            fo_ref[c, 0] = second
            fi_ref[c] = zr_ref[c, 8:10] + r32 * second
            for k in range(2):
                fix_out(c, k).start()

        @pl.when(recv_e == 3)
        def _():
            fi_ref[c] = jnp.zeros((2, 8, KP), jnp.float32)

    def stage_w(c):
        for d in (1, 2, 3):
            yc(c, d).wait_recv()

        @pl.when((recv_e == 1) | (recv_e == 2))
        def _():
            fix_in(c).wait_recv()

        mine, theirs = finish(rate(c), (m_ref[core, c, 0], m_ref[core, c, 1]), (d1_ref[c, 0], d1_ref[c, 1]),
                              across_parts(c), [yr_ref[c, d] for d in range(3)], fi_ref[c])
        w_ref[core, c, 0] = mine[0]
        w_ref[core, c, 1] = mine[1]
        ws_ref[c, 0] = theirs[0]
        ws_ref[c, 1] = theirs[1]
        d2(c).start()

    is_f = lax.broadcasted_iota(jnp.int32, (1, 8, KP), 1) < 4
    gather = [remote(me_ref.at[(z_lo + d) % 8], rows_ref.at[z_lo], ls.at[d - 1], lr.at[d - 1], others[d - 1]) for d in range(1, 8)]
    spread = [remote(back_ref.at[(z_lo + d) % 8], u_ref.at[z_lo], bs.at[d - 1], br.at[d - 1], others[d - 1]) for d in range(1, 8)]
    xcopies = [remote(total_ref, xr_ref.at[d], xs.at[d], xrs.at[d], xs_to[d]) for d in range(3)]

    def lon_totals():
        rows_ref[z_lo] = me_ref[z_lo]
        for cp in gather:
            cp.wait_recv()
        step = jnp.exp(-128.0 * inv_ref[...])
        total = jnp.zeros_like(step)
        for k in range(8):
            total = step * total + jnp.where(is_f, rows_ref[k], rows_ref[7 - k])
        total_ref[...] = total
        for cp in xcopies:
            cp.start()

    def lon_states():
        for cp in xcopies:
            cp.wait_recv()
        inv = inv_ref[...]
        step = jnp.exp(-128.0 * inv)
        r1 = jnp.exp(-1024.0 * inv)
        powers = [jnp.ones_like(r1), r1, r1 * r1]
        state = powers[2] * r1 * total_ref[...]
        for d in range(3):
            state = state + jnp.where(is_f, powers[d], powers[2 - d]) * xr_ref[d]
        states = [closing_ref[...] * state]
        for k in range(7):
            states.append(step * states[-1] + jnp.where(is_f, rows_ref[k], rows_ref[7 - k]))
        for k in range(8):
            back_ref[k] = jnp.where(is_f, states[k], states[7 - k])
        u_ref[z_lo] = back_ref[z_lo]
        for cp in spread:
            cp.start()

    def lon_moments():
        for cp in spread:
            cp.wait_recv()
        for v in range(2):
            for m in range(8):
                acc = take_ref[v, m, 0:1] * u_ref[0, v]
                for j in range(1, 8):
                    acc = acc + take_ref[v, m, j:j + 1] * u_ref[j, v]
                um_ref[v, m // 4, m % 4] = acc
        ud1.start()

    def small_own():
        return step_ref[core], (um_ref[core, 0], um_ref[core, 1]), (ud1_ref[0], ud1_ref[1])

    def small_z():
        ud1.wait_recv()
        r8, own, part = small_own()
        f, b = weigh(core == 0, r8, own, part)
        upm_ref[0] = f
        upm_ref[1] = b
        uz.start()

    def small_y():
        uz.wait_recv()
        r8 = step_ref[core]
        f, b = weigh(z_hi == 0, r8 * r8, (upm_ref[0], upm_ref[1]), (uzr_ref[0], uzr_ref[1]))
        uq_ref[0] = f
        uq_ref[1] = b
        for cp in uy:
            cp.start()

    def small_w():
        for cp in uy:
            cp.wait_recv()
        r8, own, part = small_own()
        mine, theirs = finish(r8, own, part, (uzr_ref[0], uzr_ref[1]), [uyr_ref[d] for d in range(3)])
        wu_ref[core, 0] = mine[0]
        wu_ref[core, 1] = mine[1]
        uws_ref[0] = theirs[0]
        uws_ref[1] = theirs[1]
        ud2.start()

    def early(c):
        if c > 1:
            moments(c)
        d1(c).start()

    for cp in gather:
        cp.start()
    early(0)
    early(1)
    stage_p(0)
    early(2)
    stage_p(1)
    stage_z(0)
    early(3)
    stage_p(2)
    stage_z(1)
    stage_z(2)
    lon_totals()
    early(4)
    stage_p(3)
    early(5)
    stage_p(4)
    lon_states()
    early(6)
    stage_p(5)
    early(7)
    stage_p(6)
    stage_p(7)
    late()
    stage_y(0)
    stage_z(3)
    stage_y(1)
    stage_z(4)
    stage_w(0)
    stage_f(0)
    stage_y(2)
    stage_z(5)
    stage_w(1)
    stage_y(3)
    stage_z(6)
    stage_w(2)
    stage_f(1)
    lon_moments()
    stage_y(4)
    stage_z(7)
    stage_w(3)
    stage_f(2)
    small_z()
    stage_y(5)
    stage_w(4)
    stage_f(3)
    stage_y(6)
    small_y()
    stage_w(5)
    stage_f(4)
    stage_y(7)
    small_w()
    stage_w(6)
    stage_f(5)
    carried()
    mix(0)
    stage_w(7)
    stage_f(6)
    stage_f(7)
    mix(1)

    def drain(c, carry):
        d1(c).wait_send()
        zc(c).wait_send()
        for d in (1, 2, 3):
            yc(c, d).wait_send()

        @pl.when(send_e > 0)
        def _():
            unit_out(c).wait_send()

        @pl.when(recv_e == 0)
        def _():
            for k in range(2):
                fix_out(c, k).wait_send()

        d2(c).wait_send()
        return carry

    lax.fori_loop(0, chunks, drain, 0)
    for cp in gather + xcopies + spread + [ud1, uz] + uy:
        cp.wait_send()
    ud2.wait_send()


def per_device(nlat, nlon, increment, std_dev, level_group, lon_reach, lon_weight, lat_reach, lat_weight, vertical):
    vs, levels, rows, cells = increment.shape
    f32 = jnp.float32
    vmem = pl.BlockSpec(memory_space=pltpu.VMEM)
    smem = pl.BlockSpec(memory_space=pltpu.SMEM)
    limit = 48 << 20

    dma = pltpu.SemaphoreType.DMA
    chunk = (2, 8, 8, KP)
    small = (2, 4, 8, KP)

    def scratch(*dims):
        return pltpu.VMEM(dims, f32)

    return pl.pallas_call(
        functools.partial(filter_kernel, nlat, nlon),
        out_shape=jax.ShapeDtypeStruct(increment.shape, jnp.bfloat16),
        in_specs=[smem, vmem] + [smem] * 4 + [vmem] * 3,
        out_specs=vmem,
        scratch_shapes=[
            pltpu.VMEM((1, KP), jnp.int32), scratch(4, vs, 4, 8, KP), scratch(vs, KP, KP),
            scratch(2, 8, *chunk), scratch(vs, *small), scratch(8, vs, 8, KP), scratch(vs, KP, 4 * KP), scratch(vs, 32, KP),
            scratch(vs, 4, 8, 2 * KP), scratch(vs, 8, 8, KP), scratch(vs, 8, 8, KP), pltpu.VMEM((8 * KP, KP), jnp.int32),
            scratch(vs, 8 * KP, 2 * KP), scratch(vs, 8 * KP, KP), scratch(vs, 8, KP, KP), scratch(32, KP),
            scratch(2, 8, *chunk), scratch(8, vs, 8, KP), scratch(vs, 8, 8, 8, KP), scratch(vs, 8 * KP, KP), scratch(vs, 8, 128, KP),
            scratch(vs, 4, 2, 8, KP), scratch(vs, 4, 8, KP), scratch(vs, 32, KP), scratch(vs, 8, KP), scratch(vs, 8, KP), scratch(vs, 4, 8, KP),
            scratch(vs, 8, 8, KP), scratch(vs, 5, 8, KP),
            scratch(8, *chunk), scratch(8, *chunk), scratch(8, 14, 8, KP), scratch(8, *chunk), scratch(8, 3, *chunk[1:]), scratch(8, *chunk),
            scratch(*small), scratch(vs, *small), scratch(*small), scratch(*small), scratch(*small), scratch(3, *small[1:]), scratch(*small),
            scratch(8, vs, 8, KP), scratch(vs, 8, KP), scratch(3, vs, 8, KP), scratch(8, vs, 8, KP),
            scratch(8, 14, 8, KP), scratch(8, 3, 2, 8, KP), scratch(8, 2, 2, 8, KP), scratch(8, 2, 8, KP),
            dma((9,)), dma((9,)), dma((9,)), dma((9,)), dma((9, 3)), dma((9, 3)), dma((9,)), dma((9,)),
            dma((7,)), dma((7,)), dma((3,)), dma((3,)), dma((7,)), dma((7,)), dma((8,)), dma((8, 3)), dma((8, 2)), dma((8,)),
        ],
        compiler_params=pltpu.CompilerParams(collective_id=0, has_side_effects=True, vmem_limit_bytes=limit),
        name="filter",
    )(level_group, level_group[None, :], lon_reach, lon_weight, lat_reach, lat_weight, vertical, increment, std_dev)


def solution(mesh):
    placed = (P(None, None, "lat", "lon"),) * 2 + (P(),) * 6

    def whole(increment, *rest):
        nlat, nlon = increment.shape[2:]
        body = functools.partial(per_device, nlat, nlon)
        return jax.shard_map(body, mesh=mesh, in_specs=placed, out_specs=P(None, None, "lat", "lon"), check_vma=False)(increment, *rest)

    return whole
```

```python
import functools

import jax
import jax.numpy as jnp
from jax import lax
from jax.experimental import pallas as pl
from jax.experimental.pallas import tpu as pltpu
from jax.sharding import PartitionSpec as P

KP = 128
MESH = pl.DeviceIdType.MESH


def place():
    lon = lax.axis_index("lon")
    lat = lax.axis_index("lat")
    return lon // 8, lon % 8, lat // 4, (lat // 2) % 2, lat % 2


def target(x, z_lo, y, z_hi, core):
    return {"lon": x * 8 + z_lo, "lat": y * 4 + z_hi * 2 + core}


def split(a):
    high = a.astype(jnp.bfloat16)
    return high, (a - high.astype(jnp.float32)).astype(jnp.bfloat16)


def product3(a, b, dims=(((1,), (0,)), ((), ()))):
    ah, al = split(a)
    bh, bl = split(b)
    dot = functools.partial(lax.dot_general, dimension_numbers=dims, preferred_element_type=jnp.float32)
    return dot(ah, bh) + (dot(ah, bl) + dot(al, bh))


def rise(t):
    series = 1.0 / 5040.0
    for c in (-1.0 / 720.0, 1.0 / 120.0, -1.0 / 24.0, 1.0 / 6.0, -0.5, 1.0):
        series = series * t + c
    return jnp.where(t < 0.25, t * series, 1.0 - jnp.exp(-t))


def lanes():
    return lax.broadcasted_iota(jnp.int32, (8, KP), 1)


def subs():
    return lax.broadcasted_iota(jnp.int32, (8, KP), 0)


def grouped(param_ref, kind, v, g):
    inv = 1.0 / param_ref[2 * kind, v, g]
    return inv, param_ref[2 * kind + 1, v, g] * (1.0 - jnp.exp(-inv))


def lat_gain(inv, coef, inv_all, coef_all, left):
    total = 0.0
    for q in range(4):
        both = inv + inv_all[q:q + 1]
        total = total + coef_all[q:q + 1] * (rise(both * left) / rise(both))
    return coef * total


def lat_tables(v, left_end, param_ref, take_ref, step_ref):
    j = (lanes() % 8).astype(jnp.float32)
    for g in range(4):
        inv, coef = grouped(param_ref, 1, v, g)
        take_ref[v, g, 0] = jnp.exp(-(7.0 - j) * inv)
        take_ref[v, g, 1] = jnp.exp(-j * inv) * lat_gain(inv, coef, inv, coef, left_end - j)
        step_ref[v, g] = jnp.exp(-8.0 * inv)


def lane_tables(left_end, row_ref, param_ref, edge_ref, inv8_ref, closing_ref, lane_step_ref, lane_take_ref, gain_ref, nlon):
    low = subs() < 4
    cell = lanes().astype(jnp.float32)
    row = subs().astype(jnp.float32)
    for v in range(2):
        inv8 = jnp.zeros((8, KP), jnp.float32)
        inv_k = jnp.zeros((8, KP), jnp.float32)
        coef_k = jnp.zeros((8, KP), jnp.float32)
        for g in range(4):
            inv, coef = grouped(param_ref, 1, v, g)
            inv_k = jnp.where(row_ref[...] == g, inv, inv_k)
            coef_k = jnp.where(row_ref[...] == g, coef, coef_k)
            inv, _ = grouped(param_ref, 0, v, g)
            edge_ref[v, 8 * g:8 * g + 8] = jnp.exp(-jnp.where(low, 127.0 - cell, cell) * inv)
            inv8 = jnp.where(row_ref[...] == g, inv, inv8)
        inv8_ref[v] = inv8
        closing_ref[v] = 1.0 / rise(nlon * inv8)
        for p in range(4):
            inv, coef = inv_k[p:p + 1], coef_k[p:p + 1]
            gain = lat_gain(inv, coef, inv_k, coef_k, left_end - row)
            gain_ref[v, p] = gain
            lane_step_ref[v, p] = jnp.broadcast_to(jnp.exp(-8.0 * inv), (8, KP))
            lane_take_ref[v, p] = jnp.exp(-(7.0 - row) * inv)
            lane_take_ref[v, 4 + p] = jnp.exp(-row * inv) * gain
        gain_ref[v, 4] = inv_k


def late_tables(left_end, param_ref, gain_ref, inside_ref, decay_ref, apply_ref, local_ref, give_ref):
    low = subs() < 4
    cell = lanes().astype(jnp.float32)
    row = subs().astype(jnp.float32)
    j = (lanes() % 8).astype(jnp.float32)
    part = lanes() % 64 // 16
    for v in range(2):
        for g in range(4):
            inv, coef = grouped(param_ref, 0, v, g)
            amp = 0.0
            for q in range(4):
                amp = amp + coef[q:q + 1] / rise(inv + inv[q:q + 1])
            amp = coef * amp
            decay_ref[v, 8 * g:8 * g + 8] = amp * jnp.exp(-jnp.where(low, cell + 1.0, 128.0 - cell) * inv)
            for tile in range(16):
                gap = jnp.abs(row + 8.0 * tile - cell)
                total = 0.0
                for p in range(4):
                    total = total + amp[p:p + 1] * jnp.exp(-gap * inv[p:p + 1])
                inside_ref[v, 8 * tile:8 * tile + 8, KP * g:KP * g + KP] = total
            inv, coef = grouped(param_ref, 1, v, g)
            total = 0.0
            by_lane, coef_lane = jnp.zeros((8, KP), jnp.float32), jnp.zeros((8, KP), jnp.float32)
            for p in range(4):
                gain = lat_gain(inv[p:p + 1], coef[p:p + 1], inv, coef, left_end - jnp.maximum(row, j))
                total = total + gain * jnp.exp(-jnp.abs(row - j) * inv[p:p + 1])
                by_lane = jnp.where(part == p, inv[p:p + 1], by_lane)
                coef_lane = jnp.where(part == p, coef[p:p + 1], coef_lane)
            apply_ref[v, g, :, 0:KP] = total
            gain = lat_gain(by_lane, coef_lane, inv, coef, left_end - row)
            apply_ref[v, g, :, KP:2 * KP] = jnp.where(lanes() < 64, gain * jnp.exp(-(row + 1.0) * by_lane), jnp.exp(-(8.0 - row) * by_lane))
        inv_k = gain_ref[v, 4]
        for p in range(4):
            give_ref[v, p] = gain_ref[v, p] * jnp.exp(-(row + 1.0) * inv_k[p:p + 1])
            give_ref[v, 4 + p] = jnp.exp(-(8.0 - row) * inv_k[p:p + 1])
        for i in range(8):
            total = 0.0
            for p in range(4):
                gain = jnp.where(row >= i, gain_ref[v, p], gain_ref[v, p, i:i + 1])
                total = total + gain * jnp.exp(-jnp.abs(row - i) * inv_k[p:p + 1])
            local_ref[v, i] = total


def filter_kernel(nlat, nlon, raw_group_ref, raw_row_ref, lon_reach_ref, lon_weight_ref, lat_reach_ref, lat_weight_ref, vertical_hbm,
                    inc_hbm, std_hbm, out_ref, inc_ref, std_ref, raw_vertical_ref, loads, row_ref, param_ref, vertical_ref,
                    w_ref, wu_ref, u_ref, inside_ref, decay_ref, apply_ref, local_ref, give_ref, level_ref, both_ref, y_ref, carry_ref, uz_ref,
                    m_ref, me_ref, r8_ref, x_ref, bd_ref, take_pat_ref, step_pat_ref, edge_ref, inv_ref, closing_ref, step_ref, take_ref, gain_ref,
                    d1_ref, pm_ref, zr_ref, q_ref, yr_ref, ws_ref,
                    ud1_ref, um_ref, upm_ref, uzr_ref, uq_ref, uyr_ref, uws_ref,
                    rows_ref, total_ref, xr_ref, back_ref, zo_ref, un_ref, fo_ref, fi_ref,
                    d1s, d1r, zss, zrs, yss, yrs, d2s, d2r, ls, lr, xs, xrs, bs, br, uns, unr, fos, fir):
    x, z_lo, y, z_hi, core = place()
    chunks = m_ref.shape[1]
    mate = target(x, z_lo, y, z_hi, 1 - core)
    across = target(x, z_lo, y, 1 - z_hi, core)
    ys = [target(x, z_lo, (y + d) % 4, z_hi, core) for d in (1, 2, 3)]
    xs_to = [target((x + d) % 4, z_lo, y, z_hi, core) for d in (1, 2, 3)]
    others = [target(x, (z_lo + d) % 8, y, z_hi, core) for d in range(1, 8)]
    partners = [mate, across] + ys + xs_to + others
    barrier = pltpu.get_barrier_semaphore()
    for p in partners:
        pl.semaphore_signal(barrier, inc=1, device_id=p, device_id_type=MESH)
    fetch = [(pltpu.make_async_copy(inc_hbm.at[v], inc_ref.at[v], loads.at[2 * v]), pltpu.make_async_copy(std_hbm.at[v], std_ref.at[v], loads.at[2 * v + 1]))
             for v in range(2)]
    fetch_vertical = pltpu.make_async_copy(vertical_hbm, raw_vertical_ref, loads.at[4])
    for pair in fetch:
        for cp in pair:
            cp.start()
    fetch_vertical.start()
    levels = inc_ref.shape[1]
    row_ref[:, 0:levels] = raw_row_ref[...]
    row_ref[:, levels:KP] = jnp.broadcast_to(raw_row_ref[:, levels - 1:levels], (1, KP - levels))
    part = subs() % 4
    for kind, ref in enumerate((lon_reach_ref, lon_weight_ref, lat_reach_ref, lat_weight_ref)):
        for v in range(2):
            for g in range(4):
                tile = jnp.full((8, KP), ref[v, g, 0])
                for p in range(1, 4):
                    tile = jnp.where(part == p, ref[v, g, p], tile)
                param_ref[kind, v, g] = tile

    def group_of(k):
        return raw_group_ref[jnp.minimum(k, levels - 1)]

    left_end = (nlat - 8 * lax.axis_index("lat")).astype(jnp.float32)
    starts = [jnp.sum((row_ref[...] < g).astype(jnp.int32)) for g in (1, 2, 3)]

    def prepare(v):
        lat_tables(v, left_end, param_ref, take_pat_ref, step_pat_ref)

        def build(t, carry):
            block, half = t // 2, t % 2
            level = 8 * t + subs()
            own = lanes() // 8 == 8 * half + subs()

            def choose(rows):
                tile = jnp.broadcast_to(rows[0], (8, KP))
                for g in range(1, 4):
                    tile = jnp.where(level >= starts[g - 1], rows[g], tile)
                return tile

            for p in range(4):
                r8_ref[v, block, 2 * p + half] = choose([step_pat_ref[v, g, p:p + 1] for g in range(4)])
                for part in range(2):
                    tile = choose([take_pat_ref[v, g, part, p:p + 1] for g in range(4)])
                    bd_ref[v, block, pl.ds(pl.multiple_of(part * 64 + p * 16 + half * 8, 8), 8)] = jnp.where(own, tile, 0.0)
            return carry

        lax.fori_loop(0, KP // 8, build, 0)
        for cp in fetch[v]:
            cp.wait()
        product = inc_ref[v].astype(jnp.float32) * std_ref[v].astype(jnp.float32)
        x_ref[v, pl.ds(0, levels * 8)] = product.reshape(levels * 8, KP)
        x_ref[v, pl.ds(levels * 8, 8 * (KP - levels))] = jnp.zeros((8 * (KP - levels), KP), jnp.float32)

    def moments(c):
        v = c // 4
        for half in range(2):
            block = half * 4 + c % 4
            out = product3(bd_ref[v, block], x_ref[v, pl.ds(block * 128, 128)])
            m_ref[half, c] = out.reshape(2, 8, 8, KP)

    def lon_sums():
        lane_tables(left_end, row_ref, param_ref, edge_ref, inv_ref, closing_ref, step_ref, take_ref, gain_ref, float(nlon))
        for v in range(2):
            for i in range(8):
                sums = product3(edge_ref[v], x_ref[v, pl.ds(i, KP, stride=8)], (((1,), (1,)), ((), ())))
                me_ref[i, v] = functools.reduce(jnp.add, [jnp.where(row_ref[...] == g, sums[8 * g:8 * g + 8], 0.0) for g in range(4)])
    def late():
        late_tables(left_end, param_ref, gain_ref, inside_ref, decay_ref, apply_ref, local_ref, give_ref)

        vertical_ref[...] = jnp.zeros_like(vertical_ref)
        fetch_vertical.wait()
        for v in range(2):
            vertical_ref[v, 0:levels, 0:levels] = raw_vertical_ref[:, v, :]

        def place_level(k, carry):
            g = group_of(k)
            lane = lax.broadcasted_iota(jnp.int32, (8, 2 * KP), 1)
            own = jnp.where(lane < KP, lane // 8, lane % 16) == k % 16
            rows = pl.ds(pl.multiple_of(k * 8, 8), 8)
            level_ref[rows] = jnp.full((8, KP), g, jnp.int32)
            for v in range(2):
                both_ref[v, rows] = jnp.where(own, apply_ref[v, g], 0.0)
            return carry

        lax.fori_loop(0, KP, place_level, 0)

    def stage_f(c):
        v = c // 4
        d2(c).wait_recv()
        for half in range(2):
            block = half * 4 + c % 4
            rows = pl.ds(block * 128, 128)
            source = jnp.concatenate([x_ref[v, rows], w_ref[half, c].reshape(128, KP)], axis=0)
            z = product3(both_ref[v, rows], source)
            wide = product3(z, inside_ref[v])
            result = wide[:, 0:KP]
            for g in range(1, 4):
                result = jnp.where(level_ref[rows] == g, wide[:, KP * g:KP * g + KP], result)
            y_ref[v, rows] = result

    def carried():
        ud2.wait_recv()
        for v in range(2):
            for i in range(8):
                acc = local_ref[v, i, 0:1] * u_ref[0, v]
                for j in range(1, 8):
                    acc = acc + local_ref[v, i, j:j + 1] * u_ref[j, v]
                for m in range(8):
                    acc = acc + give_ref[v, m, i:i + 1] * wu_ref[v, m // 4, m % 4]
                for g in range(4):
                    uz_ref[8 * g:8 * g + 8] = jnp.where(row_ref[...] == g, acc, 0.0)
                carry_ref[v, i] = product3(uz_ref[...], decay_ref[v], (((0,), (0,)), ((), ())))

    def mix(v):
        for i in range(8):
            rows = pl.ds(i, KP, stride=8)
            x_ref[v, rows] = product3(vertical_ref[v], y_ref[v, rows] + carry_ref[v, i])
        mixed = x_ref[v, pl.ds(0, levels * 8)].reshape(levels, 8, KP)
        out_ref[v] = (std_ref[v].astype(jnp.float32) * mixed).astype(jnp.bfloat16)

    prepare(0)
    moments(0)
    prepare(1)
    lon_sums()
    moments(1)
    pl.semaphore_wait(barrier, len(partners))

    def remote(src, dst, s, r, to):
        return pltpu.make_async_remote_copy(src_ref=src, dst_ref=dst, send_sem=s, recv_sem=r, device_id=to, device_id_type=MESH)

    def d1(c):
        return remote(m_ref.at[1 - core, c], d1_ref.at[c], d1s.at[c], d1r.at[c], mate)

    def zc(c):
        return remote(zo_ref.at[c], zr_ref.at[c], zss.at[c], zrs.at[c], across)

    send_e = jnp.where(z_hi == 0, y, 3 - y)
    recv_e = jnp.where(z_hi == 1, y, 3 - y)
    send_hub = target(x, z_lo, 3 * z_hi, z_hi, core)
    recv_to = [target(x, z_lo, jnp.where(z_hi == 1, e, 3 - e), z_hi, core) for e in (1, 2)]

    def unit_out(c):
        e = jnp.maximum(send_e, 1)
        return remote(pm_ref.at[c, 1 - z_hi, pl.ds(6, 2)], un_ref.at[c, e - 1], uns.at[c], unr.at[c, e - 1], send_hub)

    def unit_in(c, k):
        return remote(pm_ref.at[c, 1 - z_hi, pl.ds(6, 2)], un_ref.at[c, k], uns.at[c], unr.at[c, k], across)

    def fix_out(c, k):
        return remote(fo_ref.at[c, k], fi_ref.at[c], fos.at[c, k], fir.at[c], recv_to[k])

    def fix_in(c):
        return remote(fo_ref.at[c, 0], fi_ref.at[c], fos.at[c, 0], fir.at[c], across)

    def yc(c, d):
        part = (y + d) // 4
        return remote(q_ref.at[c, part], yr_ref.at[c, d - 1], yss.at[c, d - 1], yrs.at[c, d - 1], ys[d - 1])

    def d2(c):
        return remote(ws_ref.at[c], w_ref.at[core, c], d2s.at[c], d2r.at[c], mate)

    last = chunks
    ud1 = remote(um_ref.at[1 - core], ud1_ref, d1s.at[last], d1r.at[last], mate)
    uz = remote(upm_ref, uzr_ref, zss.at[last], zrs.at[last], across)
    uy = [remote(uq_ref.at[(y + d) // 4], uyr_ref.at[d - 1], yss.at[last, d - 1], yrs.at[last, d - 1], ys[d - 1]) for d in (1, 2, 3)]
    ud2 = remote(uws_ref, wu_ref.at[core], d2s.at[last], d2r.at[last], mate)

    def weigh(first, r, own, other):
        a = jnp.where(first, r, 1.0)
        b = jnp.where(first, 1.0, r)
        return a * own[0] + b * other[0], b * own[1] + a * other[1]

    def finish(r8, own, part, zr, slots, fix=None):
        r16 = r8 * r8
        r32 = r16 * r16
        powers = [jnp.ones_like(r32), r32, r32 * r32]
        wf = jnp.zeros_like(r8)
        wb = jnp.zeros_like(r8)
        for d in (1, 2, 3):
            before = y >= d
            wf = wf + jnp.where(before, powers[d - 1] * slots[d - 1], 0.0)
            wb = wb + jnp.where(before, 0.0, powers[3 - d] * slots[d - 1])
        if fix is not None:
            whole = jnp.concatenate([jnp.zeros((6, 8, KP), jnp.float32), fix], axis=0)
            wf = wf + jnp.where(z_hi == 0, whole, 0.0)
            wb = wb + jnp.where(z_hi == 0, 0.0, whole)
        lower = z_hi == 0
        wf, wb = jnp.where(lower, wf, r16 * wf + zr[0]), jnp.where(lower, r16 * wb + zr[1], wb)
        first = core == 0
        far_f, far_b = r8 * wf, r8 * wb
        mine = jnp.where(first, wf, far_f + part[0]), jnp.where(first, far_b + part[1], wb)
        theirs = jnp.where(first, far_f + own[0], wf), jnp.where(first, wb, far_b + own[1])
        return mine, theirs

    def rate(c):
        return r8_ref[c // 4, core * 4 + c % 4]

    def stage_p(c):
        d1(c).wait_recv()
        f, b = weigh(core == 0, rate(c), (m_ref[core, c, 0], m_ref[core, c, 1]), (d1_ref[c, 0], d1_ref[c, 1]))
        pm_ref[c, 0] = f
        pm_ref[c, 1] = b
        zo_ref[c, 0:8] = jnp.where(z_hi == 0, f, b)
        zo_ref[c, 8:14] = jnp.where(z_hi == 0, b, f)[0:6]

        @pl.when(send_e > 0)
        def _():
            unit_out(c).start()

    def stage_z(c):
        @pl.when(send_e == 0)
        def _():
            for k in range(3):
                unit_in(c, k).wait_recv()
                zo_ref[c, 8 + 2 * k:10 + 2 * k] = un_ref[c, k]

        zc(c).start()

    def across_parts(c):
        kept = zr_ref[c, 0:8]
        rest = jnp.concatenate([zr_ref[c, 8:14], jnp.zeros((2, 8, KP), jnp.float32)], axis=0)
        return jnp.where(z_hi == 1, kept, rest), jnp.where(z_hi == 1, rest, kept)

    def stage_y(c):
        zc(c).wait_recv()
        r8 = rate(c)
        f, b = weigh(z_hi == 0, r8 * r8, (pm_ref[c, 0], pm_ref[c, 1]), across_parts(c))
        q_ref[c, 0] = f
        q_ref[c, 1] = b
        for d in (1, 2, 3):
            yc(c, d).start()

        @pl.when(recv_e == 0)
        def _():
            r32 = r8[6:8] * r8[6:8]
            r32 = r32 * r32
            third = zr_ref[c, 12:14]
            second = zr_ref[c, 10:12] + r32 * third
            fo_ref[c, 1] = third
            fo_ref[c, 0] = second
            fi_ref[c] = zr_ref[c, 8:10] + r32 * second
            for k in range(2):
                fix_out(c, k).start()

        @pl.when(recv_e == 3)
        def _():
            fi_ref[c] = jnp.zeros((2, 8, KP), jnp.float32)

    def stage_w(c):
        for d in (1, 2, 3):
            yc(c, d).wait_recv()

        @pl.when((recv_e == 1) | (recv_e == 2))
        def _():
            fix_in(c).wait_recv()

        mine, theirs = finish(rate(c), (m_ref[core, c, 0], m_ref[core, c, 1]), (d1_ref[c, 0], d1_ref[c, 1]),
                              across_parts(c), [yr_ref[c, d] for d in range(3)], fi_ref[c])
        w_ref[core, c, 0] = mine[0]
        w_ref[core, c, 1] = mine[1]
        ws_ref[c, 0] = theirs[0]
        ws_ref[c, 1] = theirs[1]
        d2(c).start()

    is_f = lax.broadcasted_iota(jnp.int32, (1, 8, KP), 1) < 4
    gather = [remote(me_ref.at[(z_lo + d) % 8], rows_ref.at[z_lo], ls.at[d - 1], lr.at[d - 1], others[d - 1]) for d in range(1, 8)]
    spread = [remote(back_ref.at[(z_lo + d) % 8], u_ref.at[z_lo], bs.at[d - 1], br.at[d - 1], others[d - 1]) for d in range(1, 8)]
    xcopies = [remote(total_ref, xr_ref.at[d], xs.at[d], xrs.at[d], xs_to[d]) for d in range(3)]

    def lon_totals():
        rows_ref[z_lo] = me_ref[z_lo]
        for cp in gather:
            cp.wait_recv()
        step = jnp.exp(-128.0 * inv_ref[...])
        total = jnp.zeros_like(step)
        for k in range(8):
            total = step * total + jnp.where(is_f, rows_ref[k], rows_ref[7 - k])
        total_ref[...] = total
        for cp in xcopies:
            cp.start()

    def lon_states():
        for cp in xcopies:
            cp.wait_recv()
        inv = inv_ref[...]
        step = jnp.exp(-128.0 * inv)
        r1 = jnp.exp(-1024.0 * inv)
        powers = [jnp.ones_like(r1), r1, r1 * r1]
        state = powers[2] * r1 * total_ref[...]
        for d in range(3):
            state = state + jnp.where(is_f, powers[d], powers[2 - d]) * xr_ref[d]
        states = [closing_ref[...] * state]
        for k in range(7):
            states.append(step * states[-1] + jnp.where(is_f, rows_ref[k], rows_ref[7 - k]))
        for k in range(8):
            back_ref[k] = jnp.where(is_f, states[k], states[7 - k])
        u_ref[z_lo] = back_ref[z_lo]
        for cp in spread:
            cp.start()

    def lon_moments():
        for cp in spread:
            cp.wait_recv()
        for v in range(2):
            for m in range(8):
                acc = take_ref[v, m, 0:1] * u_ref[0, v]
                for j in range(1, 8):
                    acc = acc + take_ref[v, m, j:j + 1] * u_ref[j, v]
                um_ref[v, m // 4, m % 4] = acc
        ud1.start()

    def small_own():
        return step_ref[core], (um_ref[core, 0], um_ref[core, 1]), (ud1_ref[0], ud1_ref[1])

    def small_z():
        ud1.wait_recv()
        r8, own, part = small_own()
        f, b = weigh(core == 0, r8, own, part)
        upm_ref[0] = f
        upm_ref[1] = b
        uz.start()

    def small_y():
        uz.wait_recv()
        r8 = step_ref[core]
        f, b = weigh(z_hi == 0, r8 * r8, (upm_ref[0], upm_ref[1]), (uzr_ref[0], uzr_ref[1]))
        uq_ref[0] = f
        uq_ref[1] = b
        for cp in uy:
            cp.start()

    def small_w():
        for cp in uy:
            cp.wait_recv()
        r8, own, part = small_own()
        mine, theirs = finish(r8, own, part, (uzr_ref[0], uzr_ref[1]), [uyr_ref[d] for d in range(3)])
        wu_ref[core, 0] = mine[0]
        wu_ref[core, 1] = mine[1]
        uws_ref[0] = theirs[0]
        uws_ref[1] = theirs[1]
        ud2.start()

    def early(c):
        if c > 1:
            moments(c)
        d1(c).start()

    for cp in gather:
        cp.start()
    early(0)
    early(1)
    stage_p(0)
    early(2)
    stage_p(1)
    stage_z(0)
    early(3)
    stage_p(2)
    stage_z(1)
    stage_z(2)
    lon_totals()
    early(4)
    stage_p(3)
    early(5)
    stage_p(4)
    lon_states()
    early(6)
    stage_p(5)
    early(7)
    stage_p(6)
    stage_p(7)
    late()
    stage_y(0)
    stage_z(3)
    stage_y(1)
    stage_z(4)
    stage_w(0)
    stage_f(0)
    stage_y(2)
    stage_z(5)
    stage_w(1)
    stage_y(3)
    stage_z(6)
    stage_w(2)
    stage_f(1)
    lon_moments()
    stage_y(4)
    stage_z(7)
    stage_w(3)
    stage_f(2)
    small_z()
    stage_y(5)
    stage_w(4)
    stage_f(3)
    stage_y(6)
    small_y()
    stage_w(5)
    stage_f(4)
    stage_y(7)
    small_w()
    stage_w(6)
    stage_f(5)
    carried()
    mix(0)
    stage_w(7)
    stage_f(6)
    stage_f(7)
    mix(1)

    def drain(c, carry):
        d1(c).wait_send()
        zc(c).wait_send()
        for d in (1, 2, 3):
            yc(c, d).wait_send()

        @pl.when(send_e > 0)
        def _():
            unit_out(c).wait_send()

        @pl.when(recv_e == 0)
        def _():
            for k in range(2):
                fix_out(c, k).wait_send()

        d2(c).wait_send()
        return carry

    lax.fori_loop(0, chunks, drain, 0)
    for cp in gather + xcopies + spread + [ud1, uz] + uy:
        cp.wait_send()
    ud2.wait_send()


def per_device(nlat, nlon, increment, std_dev, level_group, lon_reach, lon_weight, lat_reach, lat_weight, vertical):
    vs, levels, rows, cells = increment.shape
    f32 = jnp.float32
    vmem = pl.BlockSpec(memory_space=pltpu.VMEM)
    smem = pl.BlockSpec(memory_space=pltpu.SMEM)
    limit = 63 << 20

    dma = pltpu.SemaphoreType.DMA
    chunk = (2, 8, 8, KP)
    small = (2, 4, 8, KP)

    def scratch(*dims):
        return pltpu.VMEM(dims, f32)

    return pl.pallas_call(
        functools.partial(filter_kernel, nlat, nlon),
        out_shape=jax.ShapeDtypeStruct(increment.shape, jnp.bfloat16),
        in_specs=[smem, vmem] + [smem] * 4 + [pl.BlockSpec(memory_space=pltpu.HBM)] * 3,
        out_specs=vmem,
        scratch_shapes=[
            pltpu.VMEM(increment.shape, jnp.bfloat16), pltpu.VMEM(increment.shape, jnp.bfloat16), scratch(levels, vs, levels), dma((5,)),
            pltpu.VMEM((1, KP), jnp.int32), scratch(4, vs, 4, 8, KP), scratch(vs, KP, KP),
            scratch(2, 8, *chunk), scratch(vs, *small), scratch(8, vs, 8, KP), scratch(vs, KP, 4 * KP), scratch(vs, 32, KP),
            scratch(vs, 4, 8, 2 * KP), scratch(vs, 8, 8, KP), scratch(vs, 8, 8, KP), pltpu.VMEM((8 * KP, KP), jnp.int32),
            scratch(vs, 8 * KP, 2 * KP), scratch(vs, 8 * KP, KP), scratch(vs, 8, KP, KP), scratch(32, KP),
            scratch(2, 8, *chunk), scratch(8, vs, 8, KP), scratch(vs, 8, 8, 8, KP), scratch(vs, 8 * KP, KP), scratch(vs, 8, 128, KP),
            scratch(vs, 4, 2, 8, KP), scratch(vs, 4, 8, KP), scratch(vs, 32, KP), scratch(vs, 8, KP), scratch(vs, 8, KP), scratch(vs, 4, 8, KP),
            scratch(vs, 8, 8, KP), scratch(vs, 5, 8, KP),
            scratch(8, *chunk), scratch(8, *chunk), scratch(8, 14, 8, KP), scratch(8, *chunk), scratch(8, 3, *chunk[1:]), scratch(8, *chunk),
            scratch(*small), scratch(vs, *small), scratch(*small), scratch(*small), scratch(*small), scratch(3, *small[1:]), scratch(*small),
            scratch(8, vs, 8, KP), scratch(vs, 8, KP), scratch(3, vs, 8, KP), scratch(8, vs, 8, KP),
            scratch(8, 14, 8, KP), scratch(8, 3, 2, 8, KP), scratch(8, 2, 2, 8, KP), scratch(8, 2, 8, KP),
            dma((9,)), dma((9,)), dma((9,)), dma((9,)), dma((9, 3)), dma((9, 3)), dma((9,)), dma((9,)),
            dma((7,)), dma((7,)), dma((3,)), dma((3,)), dma((7,)), dma((7,)), dma((8,)), dma((8, 3)), dma((8, 2)), dma((8,)),
        ],
        compiler_params=pltpu.CompilerParams(collective_id=0, has_side_effects=True, vmem_limit_bytes=limit),
        name="filter",
    )(level_group, level_group[None, :], lon_reach, lon_weight, lat_reach, lat_weight, jnp.transpose(vertical, (1, 0, 2)), increment, std_dev)


def solution(mesh):
    placed = (P(None, None, "lat", "lon"),) * 2 + (P(),) * 6

    def whole(increment, *rest):
        nlat, nlon = increment.shape[2:]
        body = functools.partial(per_device, nlat, nlon)
        return jax.shard_map(body, mesh=mesh, in_specs=placed, out_specs=P(None, None, "lat", "lon"), check_vma=False)(increment, *rest)

    return whole
```
